256 devices in a mesh: gx: 16 (over y_lo, z), gy: 8 (over y_hi, x), gz: 2 (over core).
Axes of the slice: x: 4, y: 4 (y_hi: 2, y_lo: 2; y = y_hi * 2 + y_lo), z: 8, core: 2. Of those that a mesh axis runs over, the one named last changes fastest.
Arguments:
- tokens: bfloat16 [128, 128, 128, 128], P('gx', 'gy', 'gz'), may hold values from -6 to 6
- w_qkv: bfloat16 [128, 384], replicated, may hold values from -0.5 to 0.5
- w_out: bfloat16 [128, 128], replicated, may hold values from -0.5 to 0.5
- w_gate_up: bfloat16 [128, 1024], replicated, may hold values from -0.5 to 0.5
- w_down: bfloat16 [512, 128], replicated, may hold values from -0.25 to 0.25
Outputs:
- updated: bfloat16 [128, 128, 128, 128], P('gx', 'gy', 'gz')
The draws below stay inside these ranges and needn't reach their ends.
All inputs are finite; a program needn't handle non-finite values.
Results may differ from the reference program's by a relative error of at most 0.014.
Values may be sent and summed in bfloat16 or wider, within the bound.
No kernel may reach another device: no remote copies, remote signals or barrier semaphores. Data moves between devices by JAX's collectives and lax.ppermute only.
A program may use at most 64 MiB of HBM per device.

```python
import math
import jax
import jax.numpy as jnp
from jax import lax

C = 128
HEADS = 8
FF = 512
LINE_X = 128
LINE_Y = 128
LINE_Z = 128


def block_scale(rng, dims, shards, least, top_value):
    level = 1.0
    for position, shards_of in shards:
        draws = jax.random.uniform(jax.random.fold_in(jax.random.fold_in(rng, 6), position), (shards_of,), jnp.float32, least / len(shards), top_value / len(shards))
        level = level * jnp.repeat(jnp.exp(draws), dims[position] // shards_of).reshape((-1,) + (1,) * (len(dims) - 1 - position))
    return level


def scatter_about(stream_key, extent, deviation, limit, cuts=(), dtype=jnp.bfloat16):
    array = deviation * jax.random.normal(stream_key, extent, jnp.float32)
    if cuts:
        array = array * block_scale(stream_key, extent, cuts, -0.22, 0.18)
    return jnp.clip(array, -limit, limit).astype(dtype)


def setup_inputs(seed: int = 0) -> dict:
    streams_of = jax.random.split(jax.random.key(seed), 6)
    tokens = scatter_about(streams_of[0], (LINE_X, LINE_Y, LINE_Z, C), 1.0, 6.0, ((0, 16), (1, 8), (2, 2)))
    w_qkv = scatter_about(streams_of[1], (C, 3 * C), C ** -0.5, 0.5)
    w_out = scatter_about(streams_of[2], (C, C), C ** -0.5, 0.5)
    w_gate_up = scatter_about(streams_of[3], (C, 2 * FF), C ** -0.5, 0.5)
    w_down = scatter_about(streams_of[4], (FF, C), FF ** -0.5, 0.25)
    return {"tokens": tokens, "w_qkv": w_qkv, "w_out": w_out, "w_gate_up": w_gate_up, "w_down": w_down}


EPS = 1e-05

def norm_rows(values):
    mean = lax.optimization_barrier(jnp.mean(values, axis=-1, keepdims=True))
    centred = values - mean
    spread = lax.optimization_barrier(jnp.mean(centred * centred, axis=-1, keepdims=True))
    return centred * lax.rsqrt(spread + EPS)

def unit_scale(values):
    return values * lax.rsqrt(jnp.mean(values * values) + 1e-06)

def make_kernel(pooled, length):
    width = pooled.shape[1] // 2
    head_dim = width // HEADS
    query = unit_scale(pooled[:, :width]).reshape(length, HEADS, head_dim)
    key_part = unit_scale(pooled[:, width:]).reshape(length, HEADS, head_dim)
    kernel = jnp.einsum('ahd,bhd->hab', query, key_part, precision=lax.Precision.HIGHEST)
    return (kernel / math.sqrt(head_dim * length)).astype(jnp.bfloat16)

def apply_first(kernel, block):
    length = block.shape[0]
    split = block.reshape(length, -1, HEADS, block.shape[-1] // HEADS).astype(jnp.float32)
    mixed = jnp.einsum('hab,bmhd->amhd', kernel.astype(jnp.float32), split)
    return mixed.reshape(block.shape)

def apply_second(kernel, block):
    split = block.reshape(block.shape[0], block.shape[1], HEADS, block.shape[-1] // HEADS).astype(jnp.float32)
    mixed = jnp.einsum('hab,ybhd->yahd', kernel.astype(jnp.float32), split)
    return mixed.reshape(block.shape)

def finish(mixed, slab, w_out, w_gate_up, w_down):
    width = slab.shape[-1]
    resid = slab.astype(jnp.float32).reshape(-1, width) + jnp.dot(mixed.reshape(-1, width), w_out, preferred_element_type=jnp.float32)
    inner = norm_rows(resid).astype(jnp.bfloat16)
    both = jnp.dot(inner, w_gate_up, preferred_element_type=jnp.float32)
    hidden = (jax.nn.gelu(both[:, :FF]) * both[:, FF:]).astype(jnp.bfloat16)
    result = resid + jnp.dot(hidden, w_down, preferred_element_type=jnp.float32)
    return result.astype(jnp.bfloat16).reshape(slab.shape)

def reference(tokens, w_qkv, w_out, w_gate_up, w_down):
    width = tokens.shape[-1]

    def project(slab):
        normed = norm_rows(slab.astype(jnp.float32)).astype(jnp.bfloat16)
        qkv = jnp.dot(normed.reshape(-1, width), w_qkv, preferred_element_type=jnp.float32)
        qkv = qkv.reshape(slab.shape[0], slab.shape[1], 3 * width)
        both = qkv[..., :2 * width]
        return (qkv[..., 2 * width:].astype(jnp.bfloat16), lax.optimization_barrier(jnp.sum(both, axis=(0, 1))), lax.optimization_barrier(jnp.sum(both, axis=1)), lax.optimization_barrier(jnp.sum(both, axis=0)))
    value, pool_x, part_y, part_z = lax.map(project, tokens)
    kernel_x = make_kernel(pool_x, LINE_X)
    kernel_y = make_kernel(lax.optimization_barrier(jnp.sum(part_y, axis=0)), LINE_Y)
    kernel_z = make_kernel(lax.optimization_barrier(jnp.sum(part_z, axis=0)), LINE_Z)

    def mix_x(block):
        return apply_first(kernel_x, block).astype(jnp.bfloat16)
    after_x = jnp.transpose(lax.map(mix_x, jnp.transpose(value, (1, 0, 2, 3))), (1, 0, 2, 3))

    def rest(pair):
        block, slab = pair
        after_y = apply_first(kernel_y, block).astype(jnp.bfloat16)
        mixed = apply_second(kernel_z, after_y).astype(jnp.bfloat16)
        return finish(mixed, slab, w_out, w_gate_up, w_down)
    return lax.map(rest, (after_x, tokens))
```

```python
import functools
import math

import jax
import jax.numpy as jnp
from jax import lax
from jax.experimental import pallas as pl
from jax.experimental.pallas import tpu as pltpu
from jax.sharding import PartitionSpec as P

HEADS = 8
HD = 16
C = 128
FF = 512
EPS = 1e-05

BF = jnp.bfloat16
F32 = jnp.float32
NT = (((1,), (1,)), ((), ()))


def dot(a, b, dims=(((1,), (0,)), ((), ()))):
    return lax.dot_general(a, b, dims, preferred_element_type=F32)


def norm_rows(values):
    mean = jnp.mean(values, axis=-1, keepdims=True)
    centred = values - mean
    spread = jnp.mean(centred * centred, axis=-1, keepdims=True)
    return centred * lax.rsqrt(spread + EPS)


def halves(values):
    high = values.astype(BF)
    low = (values - high.astype(F32)).astype(BF)
    return jnp.concatenate([high, low], axis=1)


def twice(values):
    return jnp.concatenate([values, values], axis=0)


def iota2(shape, dim):
    return lax.broadcasted_iota(jnp.int32, shape, dim)


def ones_where(cond):
    return jnp.where(cond, 1.0, 0.0).astype(BF)


def first_kernel(tok_ref, wv_ref, vt_ref, pool_ref, sx_ref, sy_acc, sz_acc):
    step = pl.program_id(0)
    _, ny, nz, _ = tok_ref.shape
    x = tok_ref[0].reshape(ny * nz, C).astype(F32)
    normed = norm_rows(x).astype(BF)
    vt = dot(wv_ref[...].T, normed, NT).astype(BF)
    vt_ref[...] = vt.reshape(HEADS, 1, HD, ny * nz)
    n32 = normed.astype(F32).reshape(ny, nz, C)
    sy = jnp.sum(n32, axis=1)
    sz = jnp.sum(n32, axis=0)

    @pl.when(step == 0)
    def _():
        sy_acc[...] = jnp.zeros_like(sy_acc)
        sz_acc[...] = jnp.zeros_like(sz_acc)

    sy_acc[...] += sy
    sz_acc[...] += sz
    sx_ref[pl.ds(step, 1), :] = jnp.sum(sy, axis=0, keepdims=True)

    @pl.when(step == pl.num_programs(0) - 1)
    def _():
        parts = pool_ref.shape[0]
        ry = ny // parts
        rz = nz // parts
        pool_ref[...] = jnp.zeros_like(pool_ref)
        pool_ref[:, 0:ry, :] = sy_acc[...].reshape(parts, ry, C)
        pool_ref[:, ry : ry + rz, :] = sz_acc[...].reshape(parts, rz, C)


def first(tokens, wv, parts):
    nx, ny, nz, _ = tokens.shape
    rows = -(-(ny // parts + nz // parts) // 8) * 8
    return pl.pallas_call(
        first_kernel,
        grid=(nx,),
        in_specs=[
            pl.BlockSpec((1, ny, nz, C), lambda i: (i, 0, 0, 0)),
            pl.BlockSpec((C, C), lambda i: (0, 0)),
        ],
        out_specs=[
            pl.BlockSpec((HEADS, 1, HD, ny * nz), lambda i: (0, i, 0, 0)),
            pl.BlockSpec((parts, rows, C), lambda i: (0, 0, 0)),
            pl.BlockSpec((nx, C), lambda i: (0, 0)),
        ],
        out_shape=[
            jax.ShapeDtypeStruct((HEADS, nx, HD, ny * nz), BF),
            jax.ShapeDtypeStruct((parts, rows, C), F32),
            jax.ShapeDtypeStruct((nx, C), F32),
        ],
        scratch_shapes=[pltpu.VMEM((ny, C), F32), pltpu.VMEM((nz, C), F32)],
        name="first",
    )(tokens, wv)


def lane_expand(rows, head, fine):
    col = iota2((C, HD * HD), 1)
    pick = (col % HD) if fine else (col // HD)
    return dot(halves(rows), twice(ones_where(iota2((C, HD * HD), 0) == head * HD + pick)))


def outer_yz(ky, kz, head):
    wide_y = lane_expand(ky, head, False)
    wide_z = lane_expand(kz, head, True)
    ny = ky.shape[0]
    nz = kz.shape[0]
    both = wide_y.reshape(ny, 1, HD * HD) * wide_z.reshape(1, nz, HD * HD)
    return both.reshape(ny * nz, HD * HD).astype(BF)


def repeat_rows(rows):
    n = rows.shape[0]
    return jnp.broadcast_to(rows.reshape(n, 1, C), (n, HD, C)).reshape(n * HD, C)


def second_kernel(
    idx_ref, r_ref, w_ref, vt_ref, send_ref, keep_ref, qo_ref, qk_scr, k_scr, *, sizes
):
    step = pl.program_id(0)
    nx, ny, nz = sizes
    px, rows, _ = r_ref.shape
    gx, gy, gz = idx_ref[0], idx_ref[1], idx_ref[2]
    py = (rows - nx) // 2
    pz = 2
    ry = ny // px
    rz = nz // px
    py = (rows - nx - pz * rz) // ry

    @pl.when(step == 0)
    def _():
        pooled = r_ref[...].reshape(px * rows, C)
        qk = dot(halves(pooled), twice(w_ref[...])).reshape(px, rows, 2 * C)
        qk_scr[...] = qk
        cuts = (0, nx, nx + py * ry, rows)
        scaled = []
        for axis in range(3):
            part = qk[:, cuts[axis] : cuts[axis + 1], :]
            length = px * (cuts[axis + 1] - cuts[axis])
            total = jnp.sum(jnp.sum(part * part, axis=0), axis=0, keepdims=True)
            mean_q = jnp.sum(total[:, :C], axis=1, keepdims=True) / (length * C)
            mean_k = jnp.sum(total[:, C:], axis=1, keepdims=True) / (length * C)
            root = 1.0 / math.sqrt(HD * length)
            scaled.append((lax.rsqrt(mean_q + 1e-06) * root, lax.rsqrt(mean_k + 1e-06)))
        own_x = qk_scr[gx, 0:nx, :]
        own_y = jnp.zeros((px, ry, 2 * C), F32)
        for g in range(py):
            at = nx + g * ry
            own_y = jnp.where(gy == g, qk[:, at : at + ry, :], own_y)
        own_y = own_y.reshape(ny, 2 * C)
        own_z = jnp.zeros((px, rz, 2 * C), F32)
        for g in range(pz):
            at = nx + py * ry + g * rz
            own_z = jnp.where(gz == g, qk[:, at : at + rz, :], own_z)
        own_z = own_z.reshape(nz, 2 * C)
        at = 0
        for own, (scale_q, scale_k) in zip((own_x, own_y, own_z), scaled):
            n = own.shape[0]
            qo_ref[at : at + n, :] = own[:, :C] * scale_q
            k_scr[at : at + n, :] = own[:, C:] * scale_k
            at += n

    half = HEADS // 2
    head = jnp.where(step < half, (1 - gz) * half + step, gz * half + step - half)
    kx = k_scr[0:nx, :]
    ky = k_scr[nx : nx + ny, :]
    kz = k_scr[nx + ny : nx + ny + nz, :]
    mixer = outer_yz(ky, kz, head)
    narrow = dot(vt_ref[0].reshape(nx * HD, ny * nz), mixer).astype(BF)
    shape = (HD * HD, C)
    pick = ones_where(iota2(shape, 1) == head * HD + iota2(shape, 0) // HD)
    spread = dot(jnp.concatenate([pick, pick], axis=1), halves(repeat_rows(kx)), NT)
    n = nx * HD
    same = iota2((HD * HD, n), 0) % HD == iota2((HD * HD, n), 1) % HD
    left = jnp.where(same, spread, 0.0).astype(BF)
    result = dot(left, narrow).astype(BF)

    @pl.when(step < half)
    def _():
        send_ref[...] = result

    @pl.when(step >= half)
    def _():
        keep_ref[...] = result


def second(idx, pooled, w_qk, vt, sizes):
    nx, ny, nz = sizes
    half = HEADS // 2
    block = HD * HD

    def head_of(i, idx_ref):
        gz = idx_ref[2]
        return jnp.where(i < half, (1 - gz) * half + i, gz * half + i - half)

    return pl.pallas_call(
        functools.partial(second_kernel, sizes=sizes),
        grid_spec=pltpu.PrefetchScalarGridSpec(
            num_scalar_prefetch=1,
            grid=(HEADS,),
            in_specs=[
                pl.BlockSpec(pooled.shape, lambda i, s: (0, 0, 0)),
                pl.BlockSpec((C, 2 * C), lambda i, s: (0, 0)),
                pl.BlockSpec((1, nx, HD, ny * nz), lambda i, s: (head_of(i, s), 0, 0, 0)),
            ],
            out_specs=[
                pl.BlockSpec((block, block), lambda i, s: (jnp.minimum(i, half - 1), 0)),
                pl.BlockSpec((block, block), lambda i, s: (jnp.maximum(i - half, 0), 0)),
                pl.BlockSpec((nx + ny + nz, C), lambda i, s: (0, 0)),
            ],
            scratch_shapes=[
                pltpu.VMEM(pooled.shape[:2] + (2 * C,), F32),
                pltpu.VMEM((nx + ny + nz, C), F32),
            ],
        ),
        out_shape=[
            jax.ShapeDtypeStruct((half * block, block), BF),
            jax.ShapeDtypeStruct((half * block, block), BF),
            jax.ShapeDtypeStruct((nx + ny + nz, C), F32),
        ],
        name="second",
    )(idx, pooled, w_qk, vt)


def third_kernel(
    idx_ref, q_ref, mine_ref, other_ref, tok_ref, wo_ref, wg_ref, wd_ref, out_ref, mix_scr, *, chunk
):
    step = pl.program_id(0)
    _, ny, nz, _ = tok_ref.shape
    nx = pl.num_programs(0)
    nx = q_ref.shape[0] - ny - nz
    half = HEADS // 2
    gz = idx_ref[2]

    @pl.when(step == 0)
    def _():
        qx = q_ref[0:nx, :]
        qy = q_ref[nx : nx + ny, :]
        qz = q_ref[nx + ny : nx + ny + nz, :]
        qx_rows = halves(repeat_rows(qx))
        n = nx * HD
        same = iota2((n, HD * HD), 0) % HD == iota2((n, HD * HD), 1) % HD
        for j in range(HEADS):
            source = mine_ref if j < half else other_ref
            head = jnp.where(gz == 0, j, (j + half) % HEADS)
            local = j % half
            mixer = outer_yz(qy, qz, head)
            shape = (C, HD * HD)
            pick = ones_where(iota2(shape, 0) == head * HD + iota2(shape, 1) // HD)
            left = jnp.where(same, dot(qx_rows, twice(pick)), 0.0).astype(BF)
            core = source[local * HD * HD : (local + 1) * HD * HD, :]
            narrow = dot(left, core).astype(BF)
            mixed = dot(narrow, mixer, NT).astype(BF)
            mix_scr[:, head, :, :] = mixed.reshape(nx, HD, ny * nz)

    mixed_t = mix_scr[step].reshape(C, ny * nz)
    mixed = mixed_t.T
    tok = tok_ref[0].reshape(ny * nz, C)
    out = []
    for at in range(0, ny * nz, chunk):
        resid = tok[at : at + chunk].astype(F32) + dot(mixed[at : at + chunk], wo_ref[...])
        inner = norm_rows(resid).astype(BF)
        both = dot(inner, wg_ref[...])
        hidden = (jax.nn.gelu(both[:, :FF]) * both[:, FF:]).astype(BF)
        result = (resid + dot(hidden, wd_ref[...])).astype(BF)
        out_ref[0, at // nz : (at + chunk) // nz] = result.reshape(chunk // nz, nz, C)


def third(idx, q, mine, other, tokens, w_out, w_gate_up, w_down):
    nx, ny, nz, _ = tokens.shape
    full = lambda a: pl.BlockSpec(a.shape, lambda i, s: (0,) * a.ndim)
    slab = pl.BlockSpec((1, ny, nz, C), lambda i, s: (i, 0, 0, 0))
    return pl.pallas_call(
        functools.partial(third_kernel, chunk=min(256, ny * nz)),
        grid_spec=pltpu.PrefetchScalarGridSpec(
            num_scalar_prefetch=1,
            grid=(nx,),
            in_specs=[
                full(q),
                full(mine),
                full(other),
                slab,
                full(w_out),
                full(w_gate_up),
                full(w_down),
            ],
            out_specs=slab,
            scratch_shapes=[pltpu.VMEM((nx, HEADS, HD, ny * nz), BF)],
        ),
        out_shape=jax.ShapeDtypeStruct(tokens.shape, BF),
        name="third",
    )(idx, q, mine, other, tokens, w_out, w_gate_up, w_down)


def a2a(values, axes):
    return lax.all_to_all(values, axes, 0, 0, tiled=True)


def body(tokens, w_qkv, w_out, w_gate_up, w_down):
    nx, ny, nz, _ = tokens.shape
    cx, cy, cz = (lax.axis_size(a) for a in ("gx", "gy", "gz"))
    idx = jnp.stack([lax.axis_index(a) for a in ("gx", "gy", "gz")]).astype(jnp.int32)
    ry = ny // cx
    rz = nz // cx
    vt, pool, sum_x = first(tokens, w_qkv[:, 2 * C :], cx)
    got = jnp.sum(a2a(pool, "gx"), axis=0)
    packed = jnp.concatenate([sum_x, got], axis=0)
    wide = jnp.broadcast_to(packed, (cy * cz,) + packed.shape)
    wide = a2a(wide, ("gy", "gz")).reshape(cy, cz, *packed.shape)
    total_x = jnp.sum(wide[:, :, :nx], axis=(0, 1))
    total_y = jnp.sum(wide[:, :, nx : nx + ry], axis=1).reshape(cy * ry, C)
    total_z = jnp.sum(wide[:, :, nx + ry : nx + ry + rz], axis=0).reshape(cz * rz, C)
    packed = jnp.concatenate([total_x, total_y, total_z], axis=0)
    pooled = a2a(jnp.broadcast_to(packed, (cx,) + packed.shape), "gx")

    send, keep, q = second(idx, pooled, w_qkv[:, : 2 * C], vt, (nx, ny, nz))
    swap = [(0, 1), (1, 0)]
    part = keep.astype(F32) + lax.ppermute(send, "gz", swap).astype(F32)
    size = cx * cy
    part = part.astype(BF).reshape(size, -1, HD * HD)
    piece = jnp.sum(a2a(part, ("gx", "gy")).astype(F32), axis=0).astype(BF)
    mine = a2a(jnp.broadcast_to(piece, (size,) + piece.shape), ("gx", "gy"))
    mine = mine.reshape(keep.shape)
    other = lax.ppermute(mine, "gz", swap)
    return third(idx, q, mine, other, tokens, w_out, w_gate_up, w_down)


def solution(mesh):
    in_specs = (P("gx", "gy", "gz", None), P(), P(), P(), P())
    out_specs = P("gx", "gy", "gz", None)
    return jax.shard_map(body, mesh=mesh, in_specs=in_specs, out_specs=out_specs, check_vma=False)
```

```python
import functools
import math

import jax
import jax.numpy as jnp
from jax import lax
from jax.experimental import pallas as pl
from jax.experimental.pallas import tpu as pltpu
from jax.sharding import PartitionSpec as P

HEADS = 8
HD = 16
C = 128
FF = 512
EPS = 1e-05

BF = jnp.bfloat16
F32 = jnp.float32
NT = (((1,), (1,)), ((), ()))


def dot(a, b, dims=(((1,), (0,)), ((), ()))):
    return lax.dot_general(a, b, dims, preferred_element_type=F32)


def norm_rows(values):
    mean = jnp.mean(values, axis=-1, keepdims=True)
    centred = values - mean
    spread = jnp.mean(centred * centred, axis=-1, keepdims=True)
    return centred * lax.rsqrt(spread + EPS)


def halves(values):
    high = values.astype(BF)
    low = (values - high.astype(F32)).astype(BF)
    return jnp.concatenate([high, low], axis=1)


def twice(values):
    return jnp.concatenate([values, values], axis=0)


def iota2(shape, dim):
    return lax.broadcasted_iota(jnp.int32, shape, dim)


def ones_where(cond):
    return jnp.where(cond, 1.0, 0.0).astype(BF)


def first_kernel(tok_ref, wv_ref, vt_ref, pool_ref, sx_ref, sy_acc, sz_acc):
    step = pl.program_id(0)
    nb, ny, nz, _ = tok_ref.shape
    x = tok_ref[...].reshape(nb * ny * nz, C).astype(F32)
    normed = norm_rows(x).astype(BF)
    wvt = wv_ref[...].T
    n32 = normed.astype(F32).reshape(nb, ny, nz, C)
    sxy = jnp.sum(n32, axis=2)
    sy = jnp.sum(sxy, axis=0)
    sz = jnp.sum(jnp.sum(n32, axis=0), axis=0)
    sx_ref[0] = jnp.sum(sxy, axis=1)
    for i in range(nb):
        vt = dot(wvt, normed[i * ny * nz : (i + 1) * ny * nz], NT).astype(BF)
        vt_ref[:, i, :, :] = vt.reshape(HEADS, HD, ny * nz)

    @pl.when(step == 0)
    def _():
        sy_acc[...] = jnp.zeros_like(sy_acc)
        sz_acc[...] = jnp.zeros_like(sz_acc)

    sy_acc[...] += sy
    sz_acc[...] += sz

    @pl.when(step == pl.num_programs(0) - 1)
    def _():
        parts = pool_ref.shape[0]
        ry = ny // parts
        rz = nz // parts
        pool_ref[...] = jnp.zeros_like(pool_ref)
        pool_ref[:, 0:ry, :] = sy_acc[...].reshape(parts, ry, C)
        pool_ref[:, ry : ry + rz, :] = sz_acc[...].reshape(parts, rz, C)


def first(tokens, w_qkv, parts, block=4):
    nx, ny, nz, _ = tokens.shape
    rows = -(-(ny // parts + nz // parts) // 8) * 8
    return pl.pallas_call(
        first_kernel,
        grid=(nx // block,),
        in_specs=[
            pl.BlockSpec((block, ny, nz, C), lambda i: (i, 0, 0, 0)),
            pl.BlockSpec((C, C), lambda i: (0, 2)),
        ],
        out_specs=[
            pl.BlockSpec((HEADS, block, HD, ny * nz), lambda i: (0, i, 0, 0)),
            pl.BlockSpec((parts, rows, C), lambda i: (0, 0, 0)),
            pl.BlockSpec((1, block, C), lambda i: (i, 0, 0)),
        ],
        out_shape=[
            jax.ShapeDtypeStruct((HEADS, nx, HD, ny * nz), BF),
            jax.ShapeDtypeStruct((parts, rows, C), F32),
            jax.ShapeDtypeStruct((nx // block, block, C), F32),
        ],
        scratch_shapes=[pltpu.VMEM((ny, C), F32), pltpu.VMEM((nz, C), F32)],
        name="first",
    )(tokens, w_qkv)


def lane_expand(rows, head, fine):
    col = iota2((C, HD * HD), 1)
    pick = (col % HD) if fine else (col // HD)
    return dot(halves(rows), twice(ones_where(iota2((C, HD * HD), 0) == head * HD + pick)))


def outer_yz(ky, kz, head):
    wide_y = lane_expand(ky, head, False)
    wide_z = lane_expand(kz, head, True)
    ny = ky.shape[0]
    nz = kz.shape[0]
    both = wide_y.reshape(ny, 1, HD * HD) * wide_z.reshape(1, nz, HD * HD)
    return both.reshape(ny * nz, HD * HD).astype(BF)


def reorder(n, major):
    out, src = iota2((n * HD, n * HD), 0), iota2((n * HD, n * HD), 1)
    cx, xc = (out, src) if major else (src, out)
    return ones_where((cx // n == xc % HD) & (cx % n == xc // HD))


def second_kernel(
    idx_ref, r_ref, w_ref, vt_ref, send_ref, keep_ref, qo_ref, kx_ref, k_scr, *, sizes
):
    step = pl.program_id(0)
    nx, ny, nz = sizes
    px, rows, _ = r_ref.shape
    gx, gy, gz = idx_ref[0], idx_ref[1], idx_ref[2]
    ry = ny // px
    rz = nz // px
    pz = 2
    py = (rows - nx - pz * rz) // ry
    half = HEADS // pz

    @pl.when(step == 0)
    def _():
        pooled = r_ref[...].reshape(px * rows, C)
        qk = dot(halves(pooled), twice(w_ref[...])).reshape(px, rows, 2 * C)
        cuts = (0, nx, nx + py * ry, rows)
        scaled = []
        for axis in range(3):
            part = qk[:, cuts[axis] : cuts[axis + 1], :]
            length = px * (cuts[axis + 1] - cuts[axis])
            total = jnp.sum(jnp.sum(part * part, axis=0), axis=0, keepdims=True)
            mean_q = jnp.sum(total[:, :C], axis=1, keepdims=True) / (length * C)
            mean_k = jnp.sum(total[:, C:], axis=1, keepdims=True) / (length * C)
            root = 1.0 / math.sqrt(HD * length)
            scaled.append((lax.rsqrt(mean_q + 1e-06) * root, lax.rsqrt(mean_k + 1e-06)))
        all_x = qk[:, 0:nx, :].reshape(px * nx, 2 * C)
        owned = gz * half + gx // (px // half)
        query = all_x[:, :C] * scaled[0][0]
        key_part = all_x[:, C:] * scaled[0][1]
        key_part = jnp.where(iota2(key_part.shape, 1) // HD == owned, key_part, 0.0)
        q_terms, k_terms = halves(query), halves(key_part)
        q_terms = jnp.concatenate([q_terms, q_terms[:, :C]], axis=1)
        k_terms = jnp.concatenate([k_terms[:, :C], k_terms[:, :C], k_terms[:, C:]], axis=1)
        kx_ref[...] = dot(q_terms, k_terms, NT).astype(BF)
        own_y = jnp.zeros((px, ry, 2 * C), F32)
        for g in range(py):
            at = nx + g * ry
            own_y = jnp.where(gy == g, qk[:, at : at + ry, :], own_y)
        own_y = own_y.reshape(ny, 2 * C)
        own_z = jnp.zeros((px, rz, 2 * C), F32)
        for g in range(pz):
            at = nx + py * ry + g * rz
            own_z = jnp.where(gz == g, qk[:, at : at + rz, :], own_z)
        own_z = own_z.reshape(nz, 2 * C)
        at = 0
        for own, (scale_q, scale_k) in zip((own_y, own_z), scaled[1:]):
            n = own.shape[0]
            qo_ref[at : at + n, :] = own[:, :C] * scale_q
            k_scr[at : at + n, :] = own[:, C:] * scale_k
            at += n

    ky = k_scr[0:ny, :]
    kz = k_scr[ny : ny + nz, :]
    perm = reorder(nx, True)
    first_head = jnp.where(step == 0, (1 - gz) * half, gz * half)

    def contract(out_ref):
        for j in range(half):
            mixer = outer_yz(ky, kz, first_head + j)
            narrow = dot(vt_ref[j].reshape(nx * HD, ny * nz), mixer).astype(BF)
            narrow = dot(perm, narrow).astype(BF).reshape(HD, nx, HD * HD)
            for side in range(2):
                cut = narrow[:, :, side * C : (side + 1) * C]
                out_ref[j * HD : (j + 1) * HD, side] = cut

    @pl.when(step == 0)
    def _():
        contract(send_ref)

    @pl.when(step == 1)
    def _():
        contract(keep_ref)


def second(idx, pooled, w_qkv, vt, sizes):
    nx, ny, nz = sizes
    half = HEADS // 2
    core = (half * HD, 2, nx, C)
    return pl.pallas_call(
        functools.partial(second_kernel, sizes=sizes),
        grid_spec=pltpu.PrefetchScalarGridSpec(
            num_scalar_prefetch=1,
            grid=(2,),
            in_specs=[
                pl.BlockSpec(memory_space=pltpu.VMEM),
                pl.BlockSpec((C, 2 * C), lambda i, s: (0, 0)),
                pl.BlockSpec(
                    (half, nx, HD, ny * nz),
                    lambda i, s: (jnp.where(i == 0, 1 - s[2], s[2]), 0, 0, 0),
                ),
            ],
            out_specs=[
                pl.BlockSpec(core, lambda i, s: (0, 0, 0, 0)),
                pl.BlockSpec(core, lambda i, s: (0, 0, 0, 0)),
                pl.BlockSpec((ny + nz, C), lambda i, s: (0, 0)),
                pl.BlockSpec((C, C), lambda i, s: (0, 0)),
            ],
            scratch_shapes=[pltpu.VMEM((ny + nz, C), F32)],
        ),
        out_shape=[
            jax.ShapeDtypeStruct(core, BF),
            jax.ShapeDtypeStruct(core, BF),
            jax.ShapeDtypeStruct((ny + nz, C), F32),
            jax.ShapeDtypeStruct((C, C), BF),
        ],
        name="second",
    )(idx, pooled, w_qkv, vt)


def middle_kernel(g_ref, kx_ref, out_ref):
    px, py, nx, _ = g_ref.shape
    lines = jnp.sum(g_ref[...].astype(F32), axis=1).reshape(px * nx, C)
    high = lines.astype(BF)
    low = (lines - high.astype(F32)).astype(BF)
    kx = kx_ref[...]
    mixed = dot(jnp.concatenate([kx, kx], axis=1), jnp.concatenate([high, low], axis=0))
    mixed = mixed.astype(BF).reshape(px, 1, nx, C)
    out_ref[...] = jnp.broadcast_to(mixed, out_ref.shape)


def middle(gathered, kx):
    vmem = pl.BlockSpec(memory_space=pltpu.VMEM)
    return pl.pallas_call(
        middle_kernel,
        in_specs=[vmem, vmem],
        out_specs=vmem,
        out_shape=jax.ShapeDtypeStruct(gathered.shape, BF),
        name="middle",
    )(gathered, kx)


def third_kernel(
    idx_ref, q_ref, mine_ref, other_ref, tok_ref, wo_ref, wg_ref, wd_ref, out_ref, mix_scr
):
    step = pl.program_id(0)
    nb, ny, nz, _ = tok_ref.shape
    nx = mix_scr.shape[0]
    half = HEADS // 2
    gz = idx_ref[2]

    @pl.when(step == 0)
    def _():
        qy = q_ref[0:ny, :]
        qz = q_ref[ny : ny + nz, :]
        perm = reorder(nx, False)
        for j in range(HEADS):
            source = mine_ref if j < half else other_ref
            head = jnp.where(gz == 0, j, (j + half) % HEADS)
            at = j % half * HD
            mixer = outer_yz(qy, qz, head)
            sides = [source[at : at + HD, i].reshape(HD * nx, C) for i in range(2)]
            narrow = dot(perm, jnp.concatenate(sides, axis=1)).astype(BF)
            mixed = dot(narrow, mixer, NT).astype(BF)
            mix_scr[:, head, :, :] = mixed.reshape(nx, HD, ny * nz)

    mixed = [mix_scr[step * nb + i].reshape(C, ny * nz).T for i in range(nb)]
    mixed = jnp.concatenate(mixed, axis=0)
    tok = tok_ref[...].reshape(nb * ny * nz, C)
    resid = tok.astype(F32) + dot(mixed, wo_ref[...])
    inner = norm_rows(resid).astype(BF)
    both = dot(inner, wg_ref[...])
    hidden = (jax.nn.gelu(both[:, :FF]) * both[:, FF:]).astype(BF)
    result = (resid + dot(hidden, wd_ref[...])).astype(BF)
    out_ref[...] = result.reshape(nb, ny, nz, C)


def third(idx, q, mine, other, tokens, w_out, w_gate_up, w_down, block=2):
    nx, ny, nz, _ = tokens.shape
    full = lambda a: pl.BlockSpec(a.shape, lambda i, s: (0,) * a.ndim)
    slab = pl.BlockSpec((block, ny, nz, C), lambda i, s: (i, 0, 0, 0))
    vmem = pl.BlockSpec(memory_space=pltpu.VMEM)
    return pl.pallas_call(
        third_kernel,
        grid_spec=pltpu.PrefetchScalarGridSpec(
            num_scalar_prefetch=1,
            grid=(nx // block,),
            in_specs=[
                full(q),
                vmem,
                vmem,
                slab,
                full(w_out),
                full(w_gate_up),
                full(w_down),
            ],
            out_specs=slab,
            scratch_shapes=[pltpu.VMEM((nx, HEADS, HD, ny * nz), BF)],
        ),
        out_shape=jax.ShapeDtypeStruct(tokens.shape, BF),
        name="third",
    )(idx, q, mine, other, tokens, w_out, w_gate_up, w_down)


def a2a(values, axes):
    return lax.all_to_all(values, axes, 0, 0, tiled=True)


def body(tokens, w_qkv, w_out, w_gate_up, w_down):
    nx, ny, nz, _ = tokens.shape
    cx, cy, cz = (lax.axis_size(a) for a in ("gx", "gy", "gz"))
    idx = jnp.stack([lax.axis_index(a) for a in ("gx", "gy", "gz")]).astype(jnp.int32)
    ry = ny // cx
    rz = nz // cx
    vt, pool, sum_x = first(tokens, w_qkv, cx)
    sum_x = sum_x.reshape(nx, C)
    got = jnp.sum(a2a(pool, "gx"), axis=0)
    packed = jnp.concatenate([sum_x, got], axis=0)
    wide = jnp.broadcast_to(packed, (cy * cz,) + packed.shape)
    wide = a2a(wide, ("gy", "gz")).reshape(cy, cz, *packed.shape)
    total_x = jnp.sum(wide[:, :, :nx], axis=(0, 1))
    total_y = jnp.sum(wide[:, :, nx : nx + ry], axis=1).reshape(cy * ry, C)
    total_z = jnp.sum(wide[:, :, nx + ry : nx + ry + rz], axis=0).reshape(cz * rz, C)
    packed = jnp.concatenate([total_x, total_y, total_z], axis=0)
    pooled = a2a(jnp.broadcast_to(packed, (cx,) + packed.shape), "gx")

    send, keep, q, kx = second(idx, pooled, w_qkv, vt, (nx, ny, nz))
    swap = [(0, 1), (1, 0)]
    part = keep.astype(F32) + lax.ppermute(send, "gz", swap).astype(F32)
    part = part.astype(BF).reshape(cx * cy, nx, C)
    gathered = a2a(part, ("gx", "gy")).reshape(cx, cy, nx, C)
    spread = middle(gathered, kx).reshape(cx * cy, nx, C)
    mine = a2a(spread, ("gx", "gy")).reshape(keep.shape)
    other = lax.ppermute(mine, "gz", swap)
    return third(idx, q, mine, other, tokens, w_out, w_gate_up, w_down)


def solution(mesh):
    in_specs = (P("gx", "gy", "gz", None), P(), P(), P(), P())
    out_specs = P("gx", "gy", "gz", None)
    return jax.shard_map(body, mesh=mesh, in_specs=in_specs, out_specs=out_specs, check_vma=False)
```

```python
import functools
import math

import jax
import jax.numpy as jnp
from jax import lax
from jax.experimental import pallas as pl
from jax.experimental.pallas import tpu as pltpu
from jax.sharding import PartitionSpec as P

HEADS = 8
HD = 16
C = 128
FF = 512
EPS = 1e-05

BF = jnp.bfloat16
F32 = jnp.float32
NT = (((1,), (1,)), ((), ()))


def dot(a, b, dims=(((1,), (0,)), ((), ()))):
    return lax.dot_general(a, b, dims, preferred_element_type=F32)


def norm_rows(values):
    mean = jnp.mean(values, axis=-1, keepdims=True)
    centred = values - mean
    spread = jnp.mean(centred * centred, axis=-1, keepdims=True)
    return centred * lax.rsqrt(spread + EPS)


def halves(values):
    high = values.astype(BF)
    low = (values - high.astype(F32)).astype(BF)
    return jnp.concatenate([high, low], axis=1)


def twice(values):
    return jnp.concatenate([values, values], axis=0)


def iota2(shape, dim):
    return lax.broadcasted_iota(jnp.int32, shape, dim)


def ones_where(cond):
    return jnp.where(cond, 1.0, 0.0).astype(BF)


def first_kernel(tok_ref, normed_ref, xy_ref, sz_ref, sx_acc, sy_acc, sz_acc):
    step = pl.program_id(0)
    nb, ny, nz, _ = tok_ref.shape
    nx = xy_ref.shape[0] - ny
    x = tok_ref[...].reshape(nb * ny * nz, C).astype(F32)
    normed = norm_rows(x).astype(BF)
    normed_ref[...] = normed.reshape(nb, ny * nz, C)
    n32 = normed.astype(F32).reshape(nb, ny, nz, C)
    sxy = jnp.sum(n32, axis=2)
    sx_acc[step] = jnp.sum(sxy, axis=1)

    @pl.when(step == 0)
    def _():
        sy_acc[...] = jnp.zeros_like(sy_acc)
        sz_acc[...] = jnp.zeros_like(sz_acc)

    sy_acc[...] += jnp.sum(sxy, axis=0)
    sz_acc[...] += jnp.sum(jnp.sum(n32, axis=0), axis=0)

    @pl.when(step == pl.num_programs(0) - 1)
    def _():
        xy_ref[0:nx, :] = sx_acc[...].reshape(nx, C)
        xy_ref[nx:, :] = sy_acc[...]
        sz_ref[...] = sz_acc[...]


def first(tokens, block=4):
    nx, ny, nz, _ = tokens.shape
    return pl.pallas_call(
        first_kernel,
        grid=(nx // block,),
        in_specs=[pl.BlockSpec((block, ny, nz, C), lambda i: (i, 0, 0, 0))],
        out_specs=[
            pl.BlockSpec((block, ny * nz, C), lambda i: (i, 0, 0)),
            pl.BlockSpec((nx + ny, C), lambda i: (0, 0)),
            pl.BlockSpec((nz, C), lambda i: (0, 0)),
        ],
        out_shape=[
            jax.ShapeDtypeStruct((nx, ny * nz, C), BF),
            jax.ShapeDtypeStruct((nx + ny, C), F32),
            jax.ShapeDtypeStruct((nz, C), F32),
        ],
        scratch_shapes=[
            pltpu.VMEM((nx // block, block, C), F32),
            pltpu.VMEM((ny, C), F32),
            pltpu.VMEM((nz, C), F32),
        ],
        name="first",
    )(tokens)


def value_kernel(normed_ref, wv_ref, vt_ref):
    wvt = wv_ref[...].T
    nb, count, _ = normed_ref.shape
    for i in range(nb):
        vt = dot(wvt, normed_ref[i], NT).astype(BF)
        vt_ref[:, i, :, :] = vt.reshape(HEADS, HD, count)


def value_of(normed, w_qkv, block=4):
    nx, count, _ = normed.shape
    return pl.pallas_call(
        value_kernel,
        grid=(nx // block,),
        in_specs=[
            pl.BlockSpec((block, count, C), lambda i: (i, 0, 0)),
            pl.BlockSpec((C, C), lambda i: (0, 2)),
        ],
        out_specs=pl.BlockSpec((HEADS, block, HD, count), lambda i: (0, i, 0, 0)),
        out_shape=jax.ShapeDtypeStruct((HEADS, nx, HD, count), BF),
        name="value",
    )(normed, w_qkv)


def in_vmem(kernel, out_shape, name, *operands):
    vmem = pl.BlockSpec(memory_space=pltpu.VMEM)
    return pl.pallas_call(
        kernel,
        in_specs=[vmem] * len(operands),
        out_specs=jax.tree.map(lambda _: vmem, out_shape),
        out_shape=out_shape,
        name=name,
    )(*operands)


def pack_y_kernel(xy_ref, got_ref, sz_ref, wide_ref, sy_ref):
    ny = sy_ref.shape[0]
    nx = xy_ref.shape[0] - ny
    both = xy_ref[...] + got_ref[...]
    sy_ref[...] = both[nx:]
    for i in range(wide_ref.shape[0]):
        wide_ref[i, 0:nx, :] = both[:nx]
        wide_ref[i, nx:, :] = sz_ref[...]


def pack_x_kernel(g_ref, sy_ref, wide_ref):
    ny = sy_ref.shape[0]
    total = jnp.sum(g_ref[...], axis=0)
    nx = wide_ref.shape[1] - ny - total.shape[0]
    nz = total.shape[0] - nx
    high = total[:nx].astype(BF)
    low = (total[:nx] - high.astype(F32)).astype(BF)
    parts = [total[nx:].astype(BF), sy_ref[...].astype(BF), high, low]
    packed = jnp.concatenate(parts, axis=0)
    for i in range(wide_ref.shape[0]):
        wide_ref[i] = packed


def lane_expand(rows, head, fine):
    col = iota2((C, HD * HD), 1)
    pick = (col % HD) if fine else (col // HD)
    return dot(halves(rows), twice(ones_where(iota2((C, HD * HD), 0) == head * HD + pick)))


def outer_yz(ky, kz, head):
    wide_y = lane_expand(ky, head, False)
    wide_z = lane_expand(kz, head, True)
    ny = ky.shape[0]
    nz = kz.shape[0]
    both = wide_y.reshape(ny, 1, HD * HD) * wide_z.reshape(1, nz, HD * HD)
    return both.reshape(ny * nz, HD * HD).astype(BF)


def reorder(n, major):
    out, src = iota2((n * HD, n * HD), 0), iota2((n * HD, n * HD), 1)
    cx, xc = (out, src) if major else (src, out)
    return ones_where((cx // n == xc % HD) & (cx % n == xc // HD))


def square_sums(rows):
    total = jnp.sum(rows * rows, axis=0, keepdims=True)
    return [jnp.sum(total[:, at : at + C], axis=1, keepdims=True) for at in (0, C)]


def second_kernel(
    idx_ref, r_ref, w_ref, vt_ref, send_ref, keep_ref, qo_ref, kx_ref, k_scr, *, sizes, count
):
    step = pl.program_id(0)
    nx, ny, nz = sizes
    px = r_ref.shape[0]
    gx, gz = idx_ref[0], idx_ref[2]
    half = HEADS // 2

    @pl.when(step == 0)
    def _():
        both = jnp.sum(r_ref[:, 0 : nz + ny, :].astype(F32), axis=0)
        terms_x = [
            r_ref[:, at : at + nx, :].reshape(px * nx, C) for at in (nz + ny, nz + ny + nx)
        ]
        weight = twice(w_ref[...])
        all_x = dot(jnp.concatenate(terms_x, axis=1), weight)
        own = dot(halves(both), weight) * (1.0 / count)
        length = px * nx
        sums = square_sums(all_x)
        query = all_x[:, :C] * lax.rsqrt(sums[0] / (length * C) + 1e-06)
        query = query * (1.0 / math.sqrt(HD * length))
        key_part = all_x[:, C:] * lax.rsqrt(sums[1] / (length * C) + 1e-06)
        owned = gz * half + gx // (px // half)
        key_part = jnp.where(iota2(key_part.shape, 1) // HD == owned, key_part, 0.0)
        q_terms, k_terms = halves(query), halves(key_part)
        q_terms = jnp.concatenate([q_terms, q_terms[:, :C]], axis=1)
        k_terms = jnp.concatenate([k_terms[:, :C], k_terms[:, :C], k_terms[:, C:]], axis=1)
        kx_ref[...] = dot(q_terms, k_terms, NT).astype(BF)
        own_z, own_y = own[:nz], own[nz:]
        qo_ref[0:ny, :] = own_y[:, :C]
        qo_ref[ny:, :] = own_z[:, :C]
        k_scr[0:ny, :] = own_y[:, C:]
        k_scr[ny:, :] = own_z[:, C:]
        lane = iota2((1, C), 1)
        row_y = jnp.zeros((1, C), F32)
        row_z = jnp.zeros((1, C), F32)
        for i, (of_y, of_z) in enumerate(zip(square_sums(own_y), square_sums(own_z))):
            for j in range(2):
                row_y = jnp.where(lane == 2 * i + j, of_y.astype(BF).astype(F32), row_y)
                at = 4 + 4 * gz + 2 * i + j
                row_z = jnp.where(lane == at, of_z.astype(BF).astype(F32), row_z)
                of_y = of_y - of_y.astype(BF).astype(F32)
                of_z = of_z - of_z.astype(BF).astype(F32)
        for ref, row in ((send_ref, row_z), (keep_ref, row_y + row_z)):
            row = jnp.broadcast_to(row.astype(BF).reshape(1, 1, 1, C), ref.shape[:2] + (nx, C))
            ref[:, :, nx:, :] = row

    ky = k_scr[0:ny, :]
    kz = k_scr[ny : ny + nz, :]
    perm = reorder(nx, True)
    first_head = jnp.where(step == 0, (1 - gz) * half, gz * half)

    def contract(out_ref):
        for j in range(half):
            mixer = outer_yz(ky, kz, first_head + j)
            narrow = dot(vt_ref[j].reshape(nx * HD, ny * nz), mixer).astype(BF)
            narrow = dot(perm, narrow).astype(BF).reshape(HD, nx, HD * HD)
            for side in range(2):
                cut = narrow[:, :, side * C : (side + 1) * C]
                out_ref[j * HD : (j + 1) * HD, side, 0:nx, :] = cut

    @pl.when(step == 0)
    def _():
        contract(send_ref)

    @pl.when(step == 1)
    def _():
        contract(keep_ref)


def second(idx, pooled, w_qkv, vt, sizes, count):
    nx, ny, nz = sizes
    half = HEADS // 2
    core = (half * HD, 2, 2 * nx, C)
    return pl.pallas_call(
        functools.partial(second_kernel, sizes=sizes, count=count),
        grid_spec=pltpu.PrefetchScalarGridSpec(
            num_scalar_prefetch=1,
            grid=(2,),
            in_specs=[
                pl.BlockSpec(memory_space=pltpu.VMEM),
                pl.BlockSpec((C, 2 * C), lambda i, s: (0, 0)),
                pl.BlockSpec(
                    (half, nx, HD, ny * nz),
                    lambda i, s: (jnp.where(i == 0, 1 - s[2], s[2]), 0, 0, 0),
                ),
            ],
            out_specs=[
                pl.BlockSpec(core, lambda i, s: (0, 0, 0, 0)),
                pl.BlockSpec(core, lambda i, s: (0, 0, 0, 0)),
                pl.BlockSpec((ny + nz, C), lambda i, s: (0, 0)),
                pl.BlockSpec((C, C), lambda i, s: (0, 0)),
            ],
            scratch_shapes=[pltpu.VMEM((ny + nz, C), F32)],
        ),
        out_shape=[
            jax.ShapeDtypeStruct(core, BF),
            jax.ShapeDtypeStruct(core, BF),
            jax.ShapeDtypeStruct((ny + nz, C), F32),
            jax.ShapeDtypeStruct((C, C), BF),
        ],
        name="second",
    )(idx, pooled, w_qkv, vt)


def middle_kernel(g_ref, kx_ref, out_ref, *, count, lengths):
    px, py, rows, _ = g_ref.shape
    nx = rows // 2
    marks = g_ref[0, :, nx, :].astype(F32)
    lane = iota2((1, C), 1)
    factor = jnp.full((1, 1), 1.0 / (HD * math.sqrt(lengths[0] * lengths[1])), F32)
    for axis, row in enumerate((jnp.sum(marks, axis=0, keepdims=True), marks[0:1])):
        for i in range(2):
            if axis == 0:
                mask = lane // 2 == i
            else:
                mask = (lane // 4 >= 1) & (lane // 4 <= 2) & (lane % 4 // 2 == i)
            total = jnp.sum(jnp.where(mask, row, 0.0), axis=1, keepdims=True)
            mean = total * (float(count) * count / (lengths[axis] * C))
            factor = factor * (lax.rsqrt(mean + 1e-06) * count)
    lines = jnp.sum(g_ref[:, :, 0:nx, :].astype(F32), axis=1).reshape(px * nx, C) * factor
    high = lines.astype(BF)
    low = (lines - high.astype(F32)).astype(BF)
    kx = kx_ref[...]
    mixed = dot(jnp.concatenate([kx, kx], axis=1), jnp.concatenate([high, low], axis=0))
    mixed = mixed.astype(BF).reshape(px, 1, nx, C)
    out_ref[...] = jnp.broadcast_to(mixed, out_ref.shape)


def third_kernel(
    idx_ref, q_ref, mine_ref, other_ref, tok_ref, wo_ref, wg_ref, wd_ref, out_ref, mix_scr
):
    step = pl.program_id(0)
    nb, ny, nz, _ = tok_ref.shape
    nx = mix_scr.shape[0]
    half = HEADS // 2
    gz = idx_ref[2]

    @pl.when(step == 0)
    def _():
        qy = q_ref[0:ny, :]
        qz = q_ref[ny : ny + nz, :]
        perm = reorder(nx, False)
        for j in range(HEADS):
            source = mine_ref if j < half else other_ref
            head = jnp.where(gz == 0, j, (j + half) % HEADS)
            at = j % half * HD
            mixer = outer_yz(qy, qz, head)
            sides = [source[at : at + HD, i].reshape(HD * nx, C) for i in range(2)]
            narrow = dot(perm, jnp.concatenate(sides, axis=1)).astype(BF)
            mixed = dot(narrow, mixer, NT).astype(BF)
            mix_scr[:, head, :, :] = mixed.reshape(nx, HD, ny * nz)

    mixed = [mix_scr[step * nb + i].reshape(C, ny * nz).T for i in range(nb)]
    mixed = jnp.concatenate(mixed, axis=0)
    tok = tok_ref[...].reshape(nb * ny * nz, C)
    resid = tok.astype(F32) + dot(mixed, wo_ref[...])
    inner = norm_rows(resid).astype(BF)
    both = dot(inner, wg_ref[...])
    hidden = (jax.nn.gelu(both[:, :FF]) * both[:, FF:]).astype(BF)
    result = (resid + dot(hidden, wd_ref[...])).astype(BF)
    out_ref[...] = result.reshape(nb, ny, nz, C)


def third(idx, q, mine, other, tokens, w_out, w_gate_up, w_down, block=2):
    nx, ny, nz, _ = tokens.shape
    full = lambda a: pl.BlockSpec(a.shape, lambda i, s: (0,) * a.ndim)
    slab = pl.BlockSpec((block, ny, nz, C), lambda i, s: (i, 0, 0, 0))
    vmem = pl.BlockSpec(memory_space=pltpu.VMEM)
    return pl.pallas_call(
        third_kernel,
        grid_spec=pltpu.PrefetchScalarGridSpec(
            num_scalar_prefetch=1,
            grid=(nx // block,),
            in_specs=[
                full(q),
                vmem,
                vmem,
                slab,
                full(w_out),
                full(w_gate_up),
                full(w_down),
            ],
            out_specs=slab,
            scratch_shapes=[pltpu.VMEM((nx, HEADS, HD, ny * nz), BF)],
        ),
        out_shape=jax.ShapeDtypeStruct(tokens.shape, BF),
        name="third",
    )(idx, q, mine, other, tokens, w_out, w_gate_up, w_down)


def a2a(values, axes):
    return lax.all_to_all(values, axes, 0, 0, tiled=True)


def body(tokens, w_qkv, w_out, w_gate_up, w_down):
    nx, ny, nz, _ = tokens.shape
    cx, cy, cz = (lax.axis_size(a) for a in ("gx", "gy", "gz"))
    idx = jnp.stack([lax.axis_index(a) for a in ("gx", "gy", "gz")]).astype(jnp.int32)
    line = nx * cx
    swap = [(0, 1), (1, 0)]
    f32 = lambda *shape: jax.ShapeDtypeStruct(shape, F32)
    bf16 = lambda *shape: jax.ShapeDtypeStruct(shape, BF)

    normed, xy, sum_z = first(tokens)
    got = lax.ppermute(xy, "gz", swap)
    wide, sum_y = in_vmem(
        pack_y_kernel, (f32(cy, nx + nz, C), f32(ny, C)), "pack_y", xy, got, sum_z
    )
    wide = a2a(wide, "gy")
    vt = value_of(normed, w_qkv)
    wide = in_vmem(pack_x_kernel, bf16(cx, nz + ny + 2 * nx, C), "pack_x", wide, sum_y)
    pooled = a2a(wide, "gx")

    send, keep, q, kx = second(idx, pooled, w_qkv, vt, (nx, ny, nz), line * line)
    part = keep.astype(F32) + lax.ppermute(send, "gz", swap).astype(F32)
    part = part.astype(BF).reshape(cx * cy, 2 * nx, C)
    gathered = a2a(part, ("gx", "gy")).reshape(cx, cy, 2 * nx, C)
    kernel = functools.partial(middle_kernel, count=line * line, lengths=(ny * cy, nz * cz))
    spread = in_vmem(kernel, bf16(cx, cy, nx, C), "middle", gathered, kx)
    mine = a2a(spread.reshape(cx * cy, nx, C), ("gx", "gy")).reshape(-1, 2, nx, C)
    other = lax.ppermute(mine, "gz", swap)
    return third(idx, q, mine, other, tokens, w_out, w_gate_up, w_down)


def solution(mesh):
    in_specs = (P("gx", "gy", "gz", None), P(), P(), P(), P())
    out_specs = P("gx", "gy", "gz", None)
    return jax.shard_map(body, mesh=mesh, in_specs=in_specs, out_specs=out_specs, check_vma=False)
```

```python
import functools
import math

import jax
import jax.numpy as jnp
from jax import lax
from jax.experimental import pallas as pl
from jax.experimental.pallas import tpu as pltpu
from jax.sharding import PartitionSpec as P

HEADS = 8
HD = 16
C = 128
FF = 512
EPS = 1e-05

BF = jnp.bfloat16
F32 = jnp.float32
NT = (((1,), (1,)), ((), ()))


def dot(a, b, dims=(((1,), (0,)), ((), ()))):
    return lax.dot_general(a, b, dims, preferred_element_type=F32)


def norm_rows(values):
    mean = jnp.mean(values, axis=-1, keepdims=True)
    centred = values - mean
    spread = jnp.mean(centred * centred, axis=-1, keepdims=True)
    return centred * lax.rsqrt(spread + EPS)


def halves(values):
    high = values.astype(BF)
    low = (values - high.astype(F32)).astype(BF)
    return jnp.concatenate([high, low], axis=1)


def twice(values):
    return jnp.concatenate([values, values], axis=0)


def iota2(shape, dim):
    return lax.broadcasted_iota(jnp.int32, shape, dim)


def ones_where(cond):
    return jnp.where(cond, 1.0, 0.0).astype(BF)


def first_kernel(tok_ref, wv_ref, vt_ref, xy_ref, sz_ref, sx_acc, sy_acc, sz_acc):
    step = pl.program_id(0)
    nb, ny, nz, _ = tok_ref.shape
    nx = xy_ref.shape[0] - ny
    x = tok_ref[...].reshape(nb * ny * nz, C).astype(F32)
    normed = norm_rows(x).astype(BF)
    wvt = wv_ref[...].T
    n32 = normed.astype(F32).reshape(nb, ny, nz, C)
    sxy = jnp.sum(n32, axis=2)
    sx_acc[step] = jnp.sum(sxy, axis=1)
    for i in range(nb):
        vt = dot(wvt, normed[i * ny * nz : (i + 1) * ny * nz], NT).astype(BF)
        vt_ref[:, i, :, :] = vt.reshape(HEADS, HD, ny * nz)

    @pl.when(step == 0)
    def _():
        sy_acc[...] = jnp.zeros_like(sy_acc)
        sz_acc[...] = jnp.zeros_like(sz_acc)

    sy_acc[...] += jnp.sum(sxy, axis=0)
    sz_acc[...] += jnp.sum(jnp.sum(n32, axis=0), axis=0)

    @pl.when(step == pl.num_programs(0) - 1)
    def _():
        xy_ref[0:nx, :] = sx_acc[...].reshape(nx, C)
        xy_ref[nx:, :] = sy_acc[...]
        sz_ref[...] = sz_acc[...]


def first(tokens, w_qkv, block=4):
    nx, ny, nz, _ = tokens.shape
    return pl.pallas_call(
        first_kernel,
        grid=(nx // block,),
        in_specs=[
            pl.BlockSpec((block, ny, nz, C), lambda i: (i, 0, 0, 0)),
            pl.BlockSpec((C, C), lambda i: (0, 2)),
        ],
        out_specs=[
            pl.BlockSpec((HEADS, block, HD, ny * nz), lambda i: (0, i, 0, 0)),
            pl.BlockSpec((nx + ny, C), lambda i: (0, 0)),
            pl.BlockSpec((nz, C), lambda i: (0, 0)),
        ],
        out_shape=[
            jax.ShapeDtypeStruct((HEADS, nx, HD, ny * nz), BF),
            jax.ShapeDtypeStruct((nx + ny, C), F32),
            jax.ShapeDtypeStruct((nz, C), F32),
        ],
        scratch_shapes=[
            pltpu.VMEM((nx // block, block, C), F32),
            pltpu.VMEM((ny, C), F32),
            pltpu.VMEM((nz, C), F32),
        ],
        name="first",
    )(tokens, w_qkv)


def in_vmem(kernel, out_shape, name, *operands):
    spaces = [pltpu.SMEM if o.dtype == jnp.int32 else pltpu.VMEM for o in operands]
    return pl.pallas_call(
        kernel,
        in_specs=[pl.BlockSpec(memory_space=space) for space in spaces],
        out_specs=pl.BlockSpec(memory_space=pltpu.VMEM),
        out_shape=out_shape,
        name=name,
    )(*operands)


def pack_kernel(idx_ref, g_ref, xy_ref, wide_ref, *, nx, cores):
    ny = xy_ref.shape[0] - nx
    count = g_ref.shape[0] // cores
    sum_x = jnp.sum(g_ref[:, 0:nx, :], axis=0)
    sum_z = jnp.sum(g_ref[:, nx + ny :, :], axis=0)
    some_y = g_ref[pl.ds(idx_ref[2] * count, count), nx : nx + ny, :]
    high = sum_x.astype(BF)
    low = (sum_x - high.astype(F32)).astype(BF)
    parts = [sum_z, xy_ref[nx:, :], some_y.reshape(count * ny, C)]
    packed = jnp.concatenate([p.astype(BF) for p in parts] + [high, low], axis=0)
    for i in range(wide_ref.shape[0]):
        wide_ref[i] = packed


def lane_expand(rows, head, fine):
    col = iota2((C, HD * HD), 1)
    pick = (col % HD) if fine else (col // HD)
    return dot(halves(rows), twice(ones_where(iota2((C, HD * HD), 0) == head * HD + pick)))


def outer_yz(ky, kz, head):
    wide_y = lane_expand(ky, head, False)
    wide_z = lane_expand(kz, head, True)
    ny = ky.shape[0]
    nz = kz.shape[0]
    both = wide_y.reshape(ny, 1, HD * HD) * wide_z.reshape(1, nz, HD * HD)
    return both.reshape(ny * nz, HD * HD).astype(BF)


def reorder(n, major):
    out, src = iota2((n * HD, n * HD), 0), iota2((n * HD, n * HD), 1)
    cx, xc = (out, src) if major else (src, out)
    return ones_where((cx // n == xc % HD) & (cx % n == xc // HD))


def square_sums(rows):
    total = jnp.sum(rows * rows, axis=0, keepdims=True)
    return [jnp.sum(total[:, at : at + C], axis=1, keepdims=True) for at in (0, C)]


def second_kernel(
    idx_ref,
    r_ref,
    w_ref,
    vt_ref,
    send_ref,
    keep_ref,
    qo_ref,
    kx_ref,
    mark_ref,
    k_scr,
    *,
    sizes,
    count
):
    step = pl.program_id(0)
    nx, ny, nz = sizes
    px, rows, _ = r_ref.shape
    gx, gz = idx_ref[0], idx_ref[2]
    half = HEADS // 2

    @pl.when(step == 0)
    def _():
        both = jnp.sum(r_ref[:, 0 : rows - 2 * nx, :].astype(F32), axis=0)
        terms_x = [
            r_ref[:, at : at + nx, :].reshape(px * nx, C) for at in (rows - 2 * nx, rows - nx)
        ]
        weight = twice(w_ref[...])
        all_x = dot(jnp.concatenate(terms_x, axis=1), weight)
        own = dot(halves(both), weight) * (1.0 / count)
        length = px * nx
        sums = square_sums(all_x)
        query = all_x[:, :C] * lax.rsqrt(sums[0] / (length * C) + 1e-06)
        query = query * (1.0 / math.sqrt(HD * length))
        key_part = all_x[:, C:] * lax.rsqrt(sums[1] / (length * C) + 1e-06)
        owned = gz * half + gx // (px // half)
        key_part = jnp.where(iota2(key_part.shape, 1) // HD == owned, key_part, 0.0)
        q_terms, k_terms = halves(query), halves(key_part)
        q_terms = jnp.concatenate([q_terms, q_terms[:, :C]], axis=1)
        k_terms = jnp.concatenate([k_terms[:, :C], k_terms[:, :C], k_terms[:, C:]], axis=1)
        kx_ref[...] = dot(q_terms, k_terms, NT).astype(BF)
        own_z, own_y, some_y = own[:nz], own[nz : nz + ny], own[nz + ny :]
        qo_ref[0:ny, :] = own_y[:, :C]
        qo_ref[ny:, :] = own_z[:, :C]
        k_scr[0:ny, :] = own_y[:, C:]
        k_scr[ny:, :] = own_z[:, C:]
        lane = iota2(mark_ref.shape, 1)
        marks = jnp.zeros(mark_ref.shape, F32)
        for i, total in enumerate(square_sums(some_y) + square_sums(own_z)):
            marks = jnp.where(lane == i, total, marks)
        mark_ref[...] = marks

    ky = k_scr[0:ny, :]
    kz = k_scr[ny : ny + nz, :]
    perm = reorder(nx, True)
    first_head = jnp.where(step == 0, (1 - gz) * half, gz * half)

    def contract(out_ref):
        for j in range(half):
            mixer = outer_yz(ky, kz, first_head + j)
            narrow = dot(vt_ref[j].reshape(nx * HD, ny * nz), mixer).astype(BF)
            narrow = dot(perm, narrow).astype(BF).reshape(HD, nx, HD * HD)
            for side in range(2):
                cut = narrow[:, :, side * C : (side + 1) * C]
                out_ref[j * HD : (j + 1) * HD, side] = cut

    @pl.when(step == 0)
    def _():
        contract(send_ref)

    @pl.when(step == 1)
    def _():
        contract(keep_ref)


def second(idx, pooled, w_qkv, vt, sizes, count):
    nx, ny, nz = sizes
    half = HEADS // 2
    core = (half * HD, 2, nx, C)
    return pl.pallas_call(
        functools.partial(second_kernel, sizes=sizes, count=count),
        grid_spec=pltpu.PrefetchScalarGridSpec(
            num_scalar_prefetch=1,
            grid=(2,),
            in_specs=[
                pl.BlockSpec(memory_space=pltpu.VMEM),
                pl.BlockSpec((C, 2 * C), lambda i, s: (0, 0)),
                pl.BlockSpec(
                    (half, nx, HD, ny * nz),
                    lambda i, s: (jnp.where(i == 0, 1 - s[2], s[2]), 0, 0, 0),
                ),
            ],
            out_specs=[
                pl.BlockSpec(core, lambda i, s: (0, 0, 0, 0)),
                pl.BlockSpec(core, lambda i, s: (0, 0, 0, 0)),
                pl.BlockSpec((ny + nz, C), lambda i, s: (0, 0)),
                pl.BlockSpec((C, C), lambda i, s: (0, 0)),
                pl.BlockSpec((8, C), lambda i, s: (0, 0)),
            ],
            scratch_shapes=[pltpu.VMEM((ny + nz, C), F32)],
        ),
        out_shape=[
            jax.ShapeDtypeStruct(core, BF),
            jax.ShapeDtypeStruct(core, BF),
            jax.ShapeDtypeStruct((ny + nz, C), F32),
            jax.ShapeDtypeStruct((C, C), BF),
            jax.ShapeDtypeStruct((8, C), F32),
        ],
        name="second",
    )(idx, pooled, w_qkv, vt)


def middle_kernel(g_ref, kx_ref, mark_ref, mark2_ref, out_ref, *, count, lengths):
    px, py, nx, _ = g_ref.shape
    marks = mark_ref[0:1, :] + mark2_ref[0:1, :]
    lane = iota2((1, C), 1)
    factor = jnp.full((1, 1), 1.0 / (HD * math.sqrt(lengths[0] * lengths[1])), F32)
    for i in range(4):
        total = jnp.sum(jnp.where(lane == i, marks, 0.0), axis=1, keepdims=True)
        mean = total * (float(count) * count / (lengths[i // 2] * C))
        factor = factor * (lax.rsqrt(mean + 1e-06) * count)
    lines = jnp.sum(g_ref[...].astype(F32), axis=1).reshape(px * nx, C) * factor
    high = lines.astype(BF)
    low = (lines - high.astype(F32)).astype(BF)
    kx = kx_ref[...]
    mixed = dot(jnp.concatenate([kx, kx], axis=1), jnp.concatenate([high, low], axis=0))
    mixed = mixed.astype(BF).reshape(px, 1, nx, C)
    out_ref[...] = jnp.broadcast_to(mixed, out_ref.shape)


def third_kernel(
    idx_ref, q_ref, mine_ref, other_ref, tok_ref, wo_ref, wg_ref, wd_ref, out_ref, mix_scr
):
    step = pl.program_id(0)
    nb, ny, nz, _ = tok_ref.shape
    nx = mix_scr.shape[0]
    half = HEADS // 2
    gz = idx_ref[2]

    @pl.when(step == 0)
    def _():
        qy = q_ref[0:ny, :]
        qz = q_ref[ny : ny + nz, :]
        perm = reorder(nx, False)
        for j in range(HEADS):
            source = mine_ref if j < half else other_ref
            head = jnp.where(gz == 0, j, (j + half) % HEADS)
            at = j % half * HD
            mixer = outer_yz(qy, qz, head)
            sides = [source[at : at + HD, i].reshape(HD * nx, C) for i in range(2)]
            narrow = dot(perm, jnp.concatenate(sides, axis=1)).astype(BF)
            mixed = dot(narrow, mixer, NT).astype(BF)
            mix_scr[:, head, :, :] = mixed.reshape(nx, HD, ny * nz)

    mixed = [mix_scr[step * nb + i].reshape(C, ny * nz).T for i in range(nb)]
    mixed = jnp.concatenate(mixed, axis=0)
    tok = tok_ref[...].reshape(nb * ny * nz, C)
    resid = tok.astype(F32) + dot(mixed, wo_ref[...])
    inner = norm_rows(resid).astype(BF)
    both = dot(inner, wg_ref[...])
    hidden = (jax.nn.gelu(both[:, :FF]) * both[:, FF:]).astype(BF)
    result = (resid + dot(hidden, wd_ref[...])).astype(BF)
    out_ref[...] = result.reshape(nb, ny, nz, C)


def third(idx, q, mine, other, tokens, w_out, w_gate_up, w_down, block=2):
    nx, ny, nz, _ = tokens.shape
    full = lambda a: pl.BlockSpec(a.shape, lambda i, s: (0,) * a.ndim)
    slab = pl.BlockSpec((block, ny, nz, C), lambda i, s: (i, 0, 0, 0))
    vmem = pl.BlockSpec(memory_space=pltpu.VMEM)
    return pl.pallas_call(
        third_kernel,
        grid_spec=pltpu.PrefetchScalarGridSpec(
            num_scalar_prefetch=1,
            grid=(nx // block,),
            in_specs=[
                full(q),
                vmem,
                vmem,
                slab,
                full(w_out),
                full(w_gate_up),
                full(w_down),
            ],
            out_specs=slab,
            scratch_shapes=[pltpu.VMEM((nx, HEADS, HD, ny * nz), BF)],
        ),
        out_shape=jax.ShapeDtypeStruct(tokens.shape, BF),
        name="third",
    )(idx, q, mine, other, tokens, w_out, w_gate_up, w_down)


def a2a(values, axes):
    return lax.all_to_all(values, axes, 0, 0, tiled=True)


def body(tokens, w_qkv, w_out, w_gate_up, w_down):
    nx, ny, nz, _ = tokens.shape
    cx, cy, cz = (lax.axis_size(a) for a in ("gx", "gy", "gz"))
    idx = jnp.stack([lax.axis_index(a) for a in ("gx", "gy", "gz")]).astype(jnp.int32)
    line = nx * cx
    swap = [(0, 1), (1, 0)]

    vt, xy, sum_z = first(tokens, w_qkv)
    xy = xy + lax.ppermute(xy, "gz", swap)
    wide, idx = lax.optimization_barrier((jnp.concatenate([xy, sum_z], axis=0), idx))
    wide = a2a(jnp.broadcast_to(wide, (cy,) + wide.shape), "gy")
    kernel = functools.partial(pack_kernel, nx=nx, cores=cz)
    shape = jax.ShapeDtypeStruct((cx, nz + ny + cy // cz * ny + 2 * nx, C), BF)
    pooled = a2a(in_vmem(kernel, shape, "pack", idx, wide, xy), "gx")

    sizes = (nx, ny, nz)
    send, keep, q, kx, marks = second(idx, pooled, w_qkv, vt, sizes, line * line)
    marks2 = lax.ppermute(marks, "gz", swap)
    part = keep.astype(F32) + lax.ppermute(send, "gz", swap).astype(F32)
    part, marks2 = lax.optimization_barrier((part.astype(BF).reshape(cx * cy, nx, C), marks2))
    gathered = a2a(part, ("gx", "gy")).reshape(cx, cy, nx, C)
    kernel = functools.partial(middle_kernel, count=line * line, lengths=(ny * cy, nz * cz))
    shape = jax.ShapeDtypeStruct(gathered.shape, BF)
    spread = in_vmem(kernel, shape, "middle", gathered, kx, marks, marks2)
    mine = a2a(spread.reshape(cx * cy, nx, C), ("gx", "gy")).reshape(-1, 2, nx, C)
    other = lax.ppermute(mine, "gz", swap)
    return third(idx, q, mine, other, tokens, w_out, w_gate_up, w_down)


def solution(mesh):
    in_specs = (P("gx", "gy", "gz", None), P(), P(), P(), P())
    out_specs = P("gx", "gy", "gz", None)
    return jax.shard_map(body, mesh=mesh, in_specs=in_specs, out_specs=out_specs, check_vma=False)
```

```python
import functools
import math

import jax
import jax.numpy as jnp
from jax import lax
from jax.experimental import pallas as pl
from jax.experimental.pallas import tpu as pltpu
from jax.sharding import PartitionSpec as P

HEADS = 8
HD = 16
C = 128
FF = 512
EPS = 1e-05

BF = jnp.bfloat16
F32 = jnp.float32
NT = (((1,), (1,)), ((), ()))


def dot(a, b, dims=(((1,), (0,)), ((), ()))):
    return lax.dot_general(a, b, dims, preferred_element_type=F32)


def dot(a, b, dims=(((1,), (0,)), ((), ()))):
    return lax.dot_general(a, b, dims, preferred_element_type=F32)


def norm_rows(values):
    mean = jnp.mean(values, axis=-1, keepdims=True)
    centred = values - mean
    spread = jnp.mean(centred * centred, axis=-1, keepdims=True)
    return centred * lax.rsqrt(spread + EPS)


def halves(values):
    high = values.astype(BF)
    low = (values - high.astype(F32)).astype(BF)
    return jnp.concatenate([high, low], axis=1)


def twice(values):
    return jnp.concatenate([values, values], axis=0)


def norm_rows_matmul(values):
    centred = values - jnp.mean(values, axis=-1, keepdims=True)
    mean_of = jnp.full((C, C), 1.0 / C, BF)
    spread = dot((centred * centred).astype(BF), mean_of)
    return centred * lax.rsqrt(spread + EPS)


def iota2(shape, dim):
    return lax.broadcasted_iota(jnp.int32, shape, dim)


def ones_where(cond):
    return jnp.where(cond, 1.0, 0.0).astype(BF)


def first_kernel(tok_ref, wv_ref, vt_ref, pool_ref, sx_ref, sy_acc, sz_acc):
    step = pl.program_id(0)
    nb, ny, nz, _ = tok_ref.shape
    x = tok_ref[...].reshape(nb * ny * nz, C).astype(F32)
    normed = norm_rows_matmul(x).astype(BF)
    wvt = wv_ref[...].T
    n32 = normed.astype(F32).reshape(nb, ny, nz, C)
    sxy = jnp.sum(n32, axis=2)
    sy = jnp.sum(sxy, axis=0)
    sz = jnp.sum(jnp.sum(n32, axis=0), axis=0)
    sx_ref[0] = jnp.sum(sxy, axis=1)
    for i in range(nb):
        vt = dot(wvt, normed[i * ny * nz : (i + 1) * ny * nz], NT).astype(BF)
        vt_ref[:, i, :, :] = vt.reshape(HEADS, HD, ny * nz)

    @pl.when(step == 0)
    def _():
        sy_acc[...] = jnp.zeros_like(sy_acc)
        sz_acc[...] = jnp.zeros_like(sz_acc)

    sy_acc[...] += sy
    sz_acc[...] += sz

    @pl.when(step == pl.num_programs(0) - 1)
    def _():
        parts = pool_ref.shape[0]
        ry = ny // parts
        rz = nz // parts
        pool_ref[...] = jnp.zeros_like(pool_ref)
        pool_ref[:, 0:ry, :] = sy_acc[...].reshape(parts, ry, C)
        pool_ref[:, ry : ry + rz, :] = sz_acc[...].reshape(parts, rz, C)


def first(tokens, w_qkv, parts, block=4):
    nx, ny, nz, _ = tokens.shape
    rows = -(-(ny // parts + nz // parts) // 8) * 8
    return pl.pallas_call(
        first_kernel,
        grid=(nx // block,),
        in_specs=[
            pl.BlockSpec((block, ny, nz, C), lambda i: (i, 0, 0, 0)),
            pl.BlockSpec((C, C), lambda i: (0, 2)),
        ],
        out_specs=[
            pl.BlockSpec((HEADS, block, HD, ny * nz), lambda i: (0, i, 0, 0)),
            pl.BlockSpec((parts, rows, C), lambda i: (0, 0, 0)),
            pl.BlockSpec((1, block, C), lambda i: (i, 0, 0)),
        ],
        out_shape=[
            jax.ShapeDtypeStruct((HEADS, nx, HD, ny * nz), BF),
            jax.ShapeDtypeStruct((parts, rows, C), F32),
            jax.ShapeDtypeStruct((nx // block, block, C), F32),
        ],
        scratch_shapes=[pltpu.VMEM((ny, C), F32), pltpu.VMEM((nz, C), F32)],
        name="first",
    )(tokens, w_qkv)


def lane_expand(rows, head, fine):
    col = iota2((C, HD * HD), 1)
    pick = (col % HD) if fine else (col // HD)
    return dot(halves(rows), twice(ones_where(iota2((C, HD * HD), 0) == head * HD + pick)))


def outer_yz(ky, kz, head):
    wide_y = lane_expand(ky, head, False)
    wide_z = lane_expand(kz, head, True)
    ny = ky.shape[0]
    nz = kz.shape[0]
    both = wide_y.reshape(ny, 1, HD * HD) * wide_z.reshape(1, nz, HD * HD)
    return both.reshape(ny * nz, HD * HD).astype(BF)


def second_kernel(
    idx_ref,
    r_ref,
    w_ref,
    vt_ref,
    send_ref,
    keep_ref,
    qo_ref,
    kx_ref,
    k_scr,
    row_scr,
    *,
    sizes
):
    step = pl.program_id(0)
    nx, ny, nz = sizes
    px, rows, _ = r_ref.shape
    gx, gy, gz = idx_ref[0], idx_ref[1], idx_ref[2]
    ry = ny // px
    rz = nz // px
    pz = 2
    py = (rows - nx - pz * rz) // ry
    half = HEADS // pz

    @pl.when(step == 0)
    def _():
        pooled = r_ref[...].reshape(px * rows, C)
        qk = dot(halves(pooled), twice(w_ref[...])).reshape(px, rows, 2 * C)
        cuts = (0, nx, nx + py * ry, rows)
        scaled = []
        for axis in range(3):
            part = qk[:, cuts[axis] : cuts[axis + 1], :]
            length = px * (cuts[axis + 1] - cuts[axis])
            total = jnp.sum(jnp.sum(part * part, axis=0), axis=0, keepdims=True)
            mean_q = jnp.sum(total[:, :C], axis=1, keepdims=True) / (length * C)
            mean_k = jnp.sum(total[:, C:], axis=1, keepdims=True) / (length * C)
            root = 1.0 / math.sqrt(HD * length)
            scaled.append((lax.rsqrt(mean_q + 1e-06) * root, lax.rsqrt(mean_k + 1e-06)))
        all_x = qk[:, 0:nx, :].reshape(px * nx, 2 * C)
        owned = gz * half + gx // (px // half)
        query = all_x[:, :C] * scaled[0][0]
        key_part = all_x[:, C:] * scaled[0][1]
        key_part = jnp.where(iota2(key_part.shape, 1) // HD == owned, key_part, 0.0)
        q_terms, k_terms = halves(query), halves(key_part)
        q_terms = jnp.concatenate([q_terms, q_terms[:, :C]], axis=1)
        k_terms = jnp.concatenate([k_terms[:, :C], k_terms[:, :C], k_terms[:, C:]], axis=1)
        kx_ref[...] = dot(q_terms, k_terms, NT).astype(BF)
        own_y = jnp.zeros((px, ry, 2 * C), F32)
        for g in range(py):
            at = nx + g * ry
            own_y = jnp.where(gy == g, qk[:, at : at + ry, :], own_y)
        own_y = own_y.reshape(ny, 2 * C)
        own_z = jnp.zeros((px, rz, 2 * C), F32)
        for g in range(pz):
            at = nx + py * ry + g * rz
            own_z = jnp.where(gz == g, qk[:, at : at + rz, :], own_z)
        own_z = own_z.reshape(nz, 2 * C)
        at = 0
        for own, (scale_q, scale_k) in zip((own_y, own_z), scaled[1:]):
            n = own.shape[0]
            qo_ref[at : at + n, :] = own[:, :C] * scale_q
            k_scr[at : at + n, :] = own[:, C:] * scale_k
            at += n

    ky = k_scr[0:ny, :]
    kz = k_scr[ny : ny + nz, :]
    first_head = jnp.where(step == 0, (1 - gz) * half, gz * half)

    def contract(out_ref):
        for j in range(half):
            mixer = outer_yz(ky, kz, first_head + j)
            narrow = dot(vt_ref[j].reshape(nx * HD, ny * nz), mixer)
            for side in range(2):
                row_scr[j, side] = narrow[:, side * C : (side + 1) * C]
                for channel in range(HD):
                    rows = row_scr[j, side, pl.ds(channel, nx, stride=HD), :]
                    out_ref[j * HD + channel, side] = rows.astype(BF)

    @pl.when(step == 0)
    def _():
        contract(send_ref)

    @pl.when(step == 1)
    def _():
        contract(keep_ref)


def second(idx, pooled, w_qkv, vt, sizes):
    nx, ny, nz = sizes
    half = HEADS // 2
    core = (half * HD, 2, nx, C)
    return pl.pallas_call(
        functools.partial(second_kernel, sizes=sizes),
        grid_spec=pltpu.PrefetchScalarGridSpec(
            num_scalar_prefetch=1,
            grid=(2,),
            in_specs=[
                pl.BlockSpec(memory_space=pltpu.VMEM),
                pl.BlockSpec((C, 2 * C), lambda i, s: (0, 0)),
                pl.BlockSpec(
                    (half, nx, HD, ny * nz),
                    lambda i, s: (jnp.where(i == 0, 1 - s[2], s[2]), 0, 0, 0),
                ),
            ],
            out_specs=[
                pl.BlockSpec(core, lambda i, s: (0, 0, 0, 0)),
                pl.BlockSpec(core, lambda i, s: (0, 0, 0, 0)),
                pl.BlockSpec((ny + nz, C), lambda i, s: (0, 0)),
                pl.BlockSpec((C, C), lambda i, s: (0, 0)),
            ],
            scratch_shapes=[
                pltpu.VMEM((ny + nz, C), F32),
                pltpu.VMEM((half, 2, nx * HD, C), F32),
            ],
        ),
        out_shape=[
            jax.ShapeDtypeStruct(core, BF),
            jax.ShapeDtypeStruct(core, BF),
            jax.ShapeDtypeStruct((ny + nz, C), F32),
            jax.ShapeDtypeStruct((C, C), BF),
        ],
        name="second",
    )(idx, pooled, w_qkv, vt)


def middle_kernel(g_ref, kx_ref, out_ref):
    px, py, nx, _ = g_ref.shape
    lines = jnp.sum(g_ref[...].astype(F32), axis=1).reshape(px * nx, C)
    high = lines.astype(BF)
    low = (lines - high.astype(F32)).astype(BF)
    kx = kx_ref[...]
    mixed = dot(jnp.concatenate([kx, kx], axis=1), jnp.concatenate([high, low], axis=0))
    mixed = mixed.astype(BF).reshape(px, 1, nx, C)
    out_ref[...] = jnp.broadcast_to(mixed, out_ref.shape)


def middle(gathered, kx):
    vmem = pl.BlockSpec(memory_space=pltpu.VMEM)
    return pl.pallas_call(
        middle_kernel,
        in_specs=[vmem, vmem],
        out_specs=vmem,
        out_shape=jax.ShapeDtypeStruct(gathered.shape, BF),
        name="middle",
    )(gathered, kx)


def third_kernel(
    idx_ref, q_ref, mine_ref, other_ref, tok_ref, wo_ref, wg_ref, wd_ref, out_ref, mix_scr, row_scr
):
    step = pl.program_id(0)
    nb, ny, nz, _ = tok_ref.shape
    nx = mix_scr.shape[0]
    half = HEADS // 2
    gz = idx_ref[2]

    @pl.when(step == 0)
    def _():
        qy = q_ref[0:ny, :]
        qz = q_ref[ny : ny + nz, :]
        for j in range(HEADS):
            source = mine_ref if j < half else other_ref
            head = jnp.where(gz == 0, j, (j + half) % HEADS)
            at = j % half * HD
            mixer = outer_yz(qy, qz, head)
            for i in range(2):
                rows = source[at : at + HD, i].astype(F32).reshape(HD * nx, C)
                row_scr[j, i] = rows
            narrow = jnp.concatenate(
                [
                    jnp.concatenate(
                        [row_scr[j, i, pl.ds(k, HD, stride=nx), :] for k in range(nx)], axis=0
                    )
                    for i in range(2)
                ],
                axis=1,
            ).astype(BF)
            mixed = dot(narrow, mixer, NT).astype(BF)
            mix_scr[:, head, :, :] = mixed.reshape(nx, HD, ny * nz)

    mixed = [mix_scr[step * nb + i].reshape(C, ny * nz).T for i in range(nb)]
    mixed = jnp.concatenate(mixed, axis=0)
    tok = tok_ref[...].reshape(nb * ny * nz, C)
    resid = tok.astype(F32) + dot(mixed, wo_ref[...])
    inner = norm_rows_matmul(resid).astype(BF)
    both = dot(inner, wg_ref[...]).astype(BF)
    gate = both[:, :FF]
    root = math.sqrt(2.0 / math.pi)
    inside = gate * (BF(root) + BF(root * 0.044715) * (gate * gate))
    half_gate = gate * BF(0.5)
    hidden = (half_gate + half_gate * jnp.tanh(inside)) * both[:, FF:]
    result = (resid + dot(hidden, wd_ref[...])).astype(BF)
    out_ref[...] = result.reshape(nb, ny, nz, C)


def third(idx, q, mine, other, tokens, w_out, w_gate_up, w_down, block=2):
    nx, ny, nz, _ = tokens.shape
    full = lambda a: pl.BlockSpec(a.shape, lambda i, s: (0,) * a.ndim)
    slab = pl.BlockSpec((block, ny, nz, C), lambda i, s: (i, 0, 0, 0))
    vmem = pl.BlockSpec(memory_space=pltpu.VMEM)
    return pl.pallas_call(
        third_kernel,
        grid_spec=pltpu.PrefetchScalarGridSpec(
            num_scalar_prefetch=1,
            grid=(nx // block,),
            in_specs=[
                full(q),
                vmem,
                vmem,
                slab,
                full(w_out),
                full(w_gate_up),
                full(w_down),
            ],
            out_specs=slab,
            scratch_shapes=[
                pltpu.VMEM((nx, HEADS, HD, ny * nz), BF),
                pltpu.VMEM((HEADS, 2, nx * HD, C), F32),
            ],
        ),
        out_shape=jax.ShapeDtypeStruct(tokens.shape, BF),
        name="third",
    )(idx, q, mine, other, tokens, w_out, w_gate_up, w_down)


def a2a(values, axes):
    return lax.all_to_all(values, axes, 0, 0, tiled=True)


def body(tokens, w_qkv, w_out, w_gate_up, w_down):
    nx, ny, nz, _ = tokens.shape
    cx, cy, cz = (lax.axis_size(a) for a in ("gx", "gy", "gz"))
    idx = jnp.stack([lax.axis_index(a) for a in ("gx", "gy", "gz")]).astype(jnp.int32)
    ry = ny // cx
    rz = nz // cx
    vt, pool, sum_x = first(tokens, w_qkv, cx)
    sum_x = sum_x.reshape(nx, C)
    pool, idx = lax.optimization_barrier((pool, idx))
    got = jnp.sum(a2a(pool, "gx"), axis=0)
    packed = jnp.concatenate([sum_x, got], axis=0)
    wide = jnp.broadcast_to(packed, (cy * cz,) + packed.shape)
    wide = a2a(wide, ("gy", "gz")).reshape(cy, cz, *packed.shape)
    total_x = jnp.sum(wide[:, :, :nx], axis=(0, 1))
    total_y = jnp.sum(wide[:, :, nx : nx + ry], axis=1).reshape(cy * ry, C)
    total_z = jnp.sum(wide[:, :, nx + ry : nx + ry + rz], axis=0).reshape(cz * rz, C)
    packed = jnp.concatenate([total_x, total_y, total_z], axis=0)
    pooled = a2a(jnp.broadcast_to(packed, (cx,) + packed.shape), "gx")

    send, keep, q, kx = second(idx, pooled, w_qkv, vt, (nx, ny, nz))
    swap = [(0, 1), (1, 0)]
    part = keep.astype(F32) + lax.ppermute(send, "gz", swap).astype(F32)
    part = part.astype(BF).reshape(cx * cy, nx, C)
    gathered = a2a(part, ("gx", "gy")).reshape(cx, cy, nx, C)
    spread = middle(gathered, kx).reshape(cx * cy, nx, C)
    mine = a2a(spread, ("gx", "gy")).reshape(keep.shape)
    other = lax.ppermute(mine, "gz", swap)
    return third(idx, q, mine, other, tokens, w_out, w_gate_up, w_down)


def solution(mesh):
    in_specs = (P("gx", "gy", "gz", None), P(), P(), P(), P())
    out_specs = P("gx", "gy", "gz", None)
    return jax.shard_map(body, mesh=mesh, in_specs=in_specs, out_specs=out_specs, check_vma=False)
```

```python
import functools
import math

import jax
import jax.numpy as jnp
from jax import lax
from jax.experimental import pallas as pl
from jax.experimental.pallas import tpu as pltpu
from jax.sharding import PartitionSpec as P

HEADS = 8
HD = 16
C = 128
FF = 512
EPS = 1e-05

BF = jnp.bfloat16
F32 = jnp.float32
NT = (((1,), (1,)), ((), ()))


def dot(a, b, dims=(((1,), (0,)), ((), ()))):
    return lax.dot_general(a, b, dims, preferred_element_type=F32)


def dot(a, b, dims=(((1,), (0,)), ((), ()))):
    return lax.dot_general(a, b, dims, preferred_element_type=F32)


def norm_rows(values):
    mean = jnp.mean(values, axis=-1, keepdims=True)
    centred = values - mean
    spread = jnp.mean(centred * centred, axis=-1, keepdims=True)
    return centred * lax.rsqrt(spread + EPS)


def halves(values):
    high = values.astype(BF)
    low = (values - high.astype(F32)).astype(BF)
    return jnp.concatenate([high, low], axis=1)


def twice(values):
    return jnp.concatenate([values, values], axis=0)


def norm_rows_matmul(values):
    centred = values - jnp.mean(values, axis=-1, keepdims=True)
    mean_of = jnp.full((C, C), 1.0 / C, BF)
    spread = dot((centred * centred).astype(BF), mean_of)
    return centred * lax.rsqrt(spread + EPS)


def iota2(shape, dim):
    return lax.broadcasted_iota(jnp.int32, shape, dim)


def ones_where(cond):
    return jnp.where(cond, 1.0, 0.0).astype(BF)


def first_kernel(
    idx_ref, tok_ref, wv_ref, keep_ref, send_ref, pool_ref, sx_ref, sy_acc, sz_acc
):
    step = pl.program_id(0)
    nb, ny, nz, _ = tok_ref.shape
    x = tok_ref[...].reshape(nb * ny * nz, C).astype(F32)
    normed = norm_rows_matmul(x).astype(BF)
    wvt = wv_ref[...].T
    n32 = normed.astype(F32).reshape(nb, ny, nz, C)
    sxy = jnp.sum(n32, axis=2)
    sy = jnp.sum(sxy, axis=0)
    sz = jnp.sum(jnp.sum(n32, axis=0), axis=0)
    sx_ref[0] = jnp.sum(sxy, axis=1)
    for i in range(nb):
        vt = dot(wvt, normed[i * ny * nz : (i + 1) * ny * nz], NT).astype(BF)
        low, high = vt[: C // 2], vt[C // 2 :]
        lower = idx_ref[2] == 0
        shape = (HEADS // 2, HD, ny * nz)
        keep_ref[:, i, :, :] = jnp.where(lower, low, high).reshape(shape)
        send_ref[:, i, :, :] = jnp.where(lower, high, low).reshape(shape)

    @pl.when(step == 0)
    def _():
        sy_acc[...] = jnp.zeros_like(sy_acc)
        sz_acc[...] = jnp.zeros_like(sz_acc)

    sy_acc[...] += sy
    sz_acc[...] += sz

    @pl.when(step == pl.num_programs(0) - 1)
    def _():
        parts = pool_ref.shape[0]
        ry = ny // parts
        rz = nz // parts
        pool_ref[...] = jnp.zeros_like(pool_ref)
        pool_ref[:, 0:ry, :] = sy_acc[...].reshape(parts, ry, C)
        pool_ref[:, ry : ry + rz, :] = sz_acc[...].reshape(parts, rz, C)


def first(idx, tokens, w_qkv, parts, block=4):
    nx, ny, nz, _ = tokens.shape
    rows = -(-(ny // parts + nz // parts) // 8) * 8
    half = HEADS // 2
    value = pl.BlockSpec((half, block, HD, ny * nz), lambda i, s: (0, i, 0, 0))
    return pl.pallas_call(
        first_kernel,
        grid_spec=pltpu.PrefetchScalarGridSpec(
            num_scalar_prefetch=1,
            grid=(nx // block,),
            in_specs=[
                pl.BlockSpec((block, ny, nz, C), lambda i, s: (i, 0, 0, 0)),
                pl.BlockSpec((C, C), lambda i, s: (0, 2)),
            ],
            out_specs=[
                value,
                value,
                pl.BlockSpec((parts, rows, C), lambda i, s: (0, 0, 0)),
                pl.BlockSpec((1, block, C), lambda i, s: (i, 0, 0)),
            ],
            scratch_shapes=[pltpu.VMEM((ny, C), F32), pltpu.VMEM((nz, C), F32)],
        ),
        out_shape=[
            jax.ShapeDtypeStruct((half, nx, HD, ny * nz), BF),
            jax.ShapeDtypeStruct((half, nx, HD, ny * nz), BF),
            jax.ShapeDtypeStruct((parts, rows, C), F32),
            jax.ShapeDtypeStruct((nx // block, block, C), F32),
        ],
        name="first",
    )(idx, tokens, w_qkv)


def lane_expand(rows, head, fine):
    col = iota2((C, HD * HD), 1)
    pick = (col % HD) if fine else (col // HD)
    return dot(halves(rows), twice(ones_where(iota2((C, HD * HD), 0) == head * HD + pick)))


def outer_yz(ky, kz, head):
    wide_y = lane_expand(ky, head, False)
    wide_z = lane_expand(kz, head, True)
    ny = ky.shape[0]
    nz = kz.shape[0]
    both = wide_y.reshape(ny, 1, HD * HD) * wide_z.reshape(1, nz, HD * HD)
    return both.reshape(ny * nz, HD * HD).astype(BF)


def second_kernel(
    idx_ref,
    r_ref,
    w_ref,
    mine_ref,
    got_ref,
    out_ref,
    qo_ref,
    kx_ref,
    k_scr,
    row_scr,
    *,
    sizes
):
    step = pl.program_id(0)
    nx, ny, nz = sizes
    px, rows, _ = r_ref.shape
    gx, gy, gz = idx_ref[0], idx_ref[1], idx_ref[2]
    ry = ny // px
    rz = nz // px
    pz = 2
    py = (rows - nx - pz * rz) // ry
    half = HEADS // pz

    @pl.when(step == 0)
    def _():
        pooled = r_ref[...].reshape(px * rows, C)
        qk = dot(halves(pooled), twice(w_ref[...])).reshape(px, rows, 2 * C)
        cuts = (0, nx, nx + py * ry, rows)
        scaled = []
        for axis in range(3):
            part = qk[:, cuts[axis] : cuts[axis + 1], :]
            length = px * (cuts[axis + 1] - cuts[axis])
            total = jnp.sum(jnp.sum(part * part, axis=0), axis=0, keepdims=True)
            mean_q = jnp.sum(total[:, :C], axis=1, keepdims=True) / (length * C)
            mean_k = jnp.sum(total[:, C:], axis=1, keepdims=True) / (length * C)
            root = 1.0 / math.sqrt(HD * length)
            scaled.append((lax.rsqrt(mean_q + 1e-06) * root, lax.rsqrt(mean_k + 1e-06)))
        all_x = qk[:, 0:nx, :].reshape(px * nx, 2 * C)
        owned = gz * half + gx // (px // half)
        query = all_x[:, :C] * scaled[0][0]
        key_part = all_x[:, C:] * scaled[0][1]
        key_part = jnp.where(iota2(key_part.shape, 1) // HD == owned, key_part, 0.0)
        q_terms, k_terms = halves(query), halves(key_part)
        q_terms = jnp.concatenate([q_terms, q_terms[:, :C]], axis=1)
        k_terms = jnp.concatenate([k_terms[:, :C], k_terms[:, :C], k_terms[:, C:]], axis=1)
        kx_ref[...] = dot(q_terms, k_terms, NT).astype(BF)
        own_y = jnp.zeros((px, ry, 2 * C), F32)
        for g in range(py):
            at = nx + g * ry
            own_y = jnp.where(gy == g, qk[:, at : at + ry, :], own_y)
        own_y = own_y.reshape(ny, 2 * C)
        at = nx + py * ry
        low = qk[:, at : at + rz, :].reshape(nz, 2 * C)
        high = qk[:, at + rz : at + 2 * rz, :].reshape(nz, 2 * C)
        own_z = jnp.where(gz == 0, low, high)
        other_z = jnp.where(gz == 0, high, low)
        qo_ref[0:ny, :] = own_y[:, :C] * scaled[1][0]
        qo_ref[ny:, :] = own_z[:, :C] * scaled[2][0]
        k_scr[0:ny, :] = own_y[:, C:] * scaled[1][1]
        k_scr[ny : ny + nz, :] = own_z[:, C:] * scaled[2][1]
        k_scr[ny + nz :, :] = other_z[:, C:] * scaled[2][1]

    heads = mine_ref.shape[0]
    for j in range(heads):
        head = gz * half + step * heads + j
        wide_y = lane_expand(k_scr[0:ny, :], head, False).reshape(ny, 1, HD * HD)
        wide_z = lane_expand(k_scr[ny:, :], head, True)
        narrow = jnp.zeros((nx * HD, HD * HD), F32)
        for i, source in enumerate((mine_ref, got_ref)):
            mixer = wide_y * wide_z[i * nz : (i + 1) * nz].reshape(1, nz, HD * HD)
            mixer = mixer.reshape(ny * nz, HD * HD).astype(BF)
            narrow = narrow + dot(source[j].reshape(nx * HD, ny * nz), mixer)
        for side in range(2):
            row_scr[j, side] = narrow[:, side * C : (side + 1) * C]
            for channel in range(HD):
                rows = row_scr[j, side, pl.ds(channel, nx, stride=HD), :]
                out_ref[j * HD + channel, side] = rows.astype(BF)


def second(idx, pooled, w_qkv, mine, got, sizes, steps=2):
    nx, ny, nz = sizes
    half = HEADS // 2
    heads = half // steps
    value = pl.BlockSpec((heads, nx, HD, ny * nz), lambda i, s: (i, 0, 0, 0))
    return pl.pallas_call(
        functools.partial(second_kernel, sizes=sizes),
        grid_spec=pltpu.PrefetchScalarGridSpec(
            num_scalar_prefetch=1,
            grid=(steps,),
            in_specs=[
                pl.BlockSpec(memory_space=pltpu.VMEM),
                pl.BlockSpec((C, 2 * C), lambda i, s: (0, 0)),
                value,
                value,
            ],
            out_specs=[
                pl.BlockSpec((heads * HD, 2, nx, C), lambda i, s: (i, 0, 0, 0)),
                pl.BlockSpec((ny + nz, C), lambda i, s: (0, 0)),
                pl.BlockSpec((C, C), lambda i, s: (0, 0)),
            ],
            scratch_shapes=[
                pltpu.VMEM((ny + 2 * nz, C), F32),
                pltpu.VMEM((heads, 2, nx * HD, C), F32),
            ],
        ),
        out_shape=[
            jax.ShapeDtypeStruct((half * HD, 2, nx, C), BF),
            jax.ShapeDtypeStruct((ny + nz, C), F32),
            jax.ShapeDtypeStruct((C, C), BF),
        ],
        name="second",
    )(idx, pooled, w_qkv, mine, got)


def middle_kernel(g_ref, kx_ref, out_ref):
    px, py, nx, _ = g_ref.shape
    lines = jnp.sum(g_ref[...].astype(F32), axis=1).reshape(px * nx, C)
    high = lines.astype(BF)
    low = (lines - high.astype(F32)).astype(BF)
    kx = kx_ref[...]
    mixed = dot(jnp.concatenate([kx, kx], axis=1), jnp.concatenate([high, low], axis=0))
    mixed = mixed.astype(BF).reshape(px, 1, nx, C)
    out_ref[...] = jnp.broadcast_to(mixed, out_ref.shape)


def middle(gathered, kx):
    vmem = pl.BlockSpec(memory_space=pltpu.VMEM)
    return pl.pallas_call(
        middle_kernel,
        in_specs=[vmem, vmem],
        out_specs=vmem,
        out_shape=jax.ShapeDtypeStruct(gathered.shape, BF),
        name="middle",
    )(gathered, kx)


def third_kernel(
    idx_ref, q_ref, mine_ref, other_ref, tok_ref, wo_ref, wg_ref, wd_ref, out_ref, mix_scr, row_scr
):
    step = pl.program_id(0)
    nb, ny, nz, _ = tok_ref.shape
    nx = mix_scr.shape[0]
    half = HEADS // 2
    gz = idx_ref[2]

    @pl.when(step == 0)
    def _():
        qy = q_ref[0:ny, :]
        qz = q_ref[ny : ny + nz, :]
        for j in range(HEADS):
            source = mine_ref if j < half else other_ref
            head = jnp.where(gz == 0, j, (j + half) % HEADS)
            at = j % half * HD
            mixer = outer_yz(qy, qz, head)
            for i in range(2):
                rows = source[at : at + HD, i].astype(F32).reshape(HD * nx, C)
                row_scr[j, i] = rows
            narrow = jnp.concatenate(
                [
                    jnp.concatenate(
                        [row_scr[j, i, pl.ds(k, HD, stride=nx), :] for k in range(nx)], axis=0
                    )
                    for i in range(2)
                ],
                axis=1,
            ).astype(BF)
            mixed = dot(narrow, mixer, NT).astype(BF)
            mix_scr[:, head, :, :] = mixed.reshape(nx, HD, ny * nz)

    mixed = [mix_scr[step * nb + i].reshape(C, ny * nz).T for i in range(nb)]
    mixed = jnp.concatenate(mixed, axis=0)
    tok = tok_ref[...].reshape(nb * ny * nz, C)
    resid = tok.astype(F32) + dot(mixed, wo_ref[...])
    inner = norm_rows_matmul(resid).astype(BF)
    both = dot(inner, wg_ref[...]).astype(BF)
    gate = both[:, :FF]
    root = math.sqrt(2.0 / math.pi)
    inside = gate * (BF(root) + BF(root * 0.044715) * (gate * gate))
    half_gate = gate * BF(0.5)
    hidden = (half_gate + half_gate * jnp.tanh(inside)) * both[:, FF:]
    result = (resid + dot(hidden, wd_ref[...])).astype(BF)
    out_ref[...] = result.reshape(nb, ny, nz, C)


def third(idx, q, mine, other, tokens, w_out, w_gate_up, w_down, block=2):
    nx, ny, nz, _ = tokens.shape
    full = lambda a: pl.BlockSpec(a.shape, lambda i, s: (0,) * a.ndim)
    slab = pl.BlockSpec((block, ny, nz, C), lambda i, s: (i, 0, 0, 0))
    vmem = pl.BlockSpec(memory_space=pltpu.VMEM)
    return pl.pallas_call(
        third_kernel,
        grid_spec=pltpu.PrefetchScalarGridSpec(
            num_scalar_prefetch=1,
            grid=(nx // block,),
            in_specs=[
                full(q),
                vmem,
                vmem,
                slab,
                full(w_out),
                full(w_gate_up),
                full(w_down),
            ],
            out_specs=slab,
            scratch_shapes=[
                pltpu.VMEM((nx, HEADS, HD, ny * nz), BF),
                pltpu.VMEM((HEADS, 2, nx * HD, C), F32),
            ],
        ),
        out_shape=jax.ShapeDtypeStruct(tokens.shape, BF),
        name="third",
    )(idx, q, mine, other, tokens, w_out, w_gate_up, w_down)


def a2a(values, axes):
    return lax.all_to_all(values, axes, 0, 0, tiled=True)


def body(tokens, w_qkv, w_out, w_gate_up, w_down):
    nx, ny, nz, _ = tokens.shape
    cx, cy, cz = (lax.axis_size(a) for a in ("gx", "gy", "gz"))
    idx = jnp.stack([lax.axis_index(a) for a in ("gx", "gy", "gz")]).astype(jnp.int32)
    ry = ny // cx
    rz = nz // cx
    keep, send, pool, sum_x = first(idx, tokens, w_qkv, cx)
    got_value = lax.ppermute(send, "gz", [(0, 1), (1, 0)])
    sum_x = sum_x.reshape(nx, C)
    got = jnp.sum(a2a(pool, "gx"), axis=0)
    packed = jnp.concatenate([sum_x, got], axis=0)
    wide = jnp.broadcast_to(packed, (cy * cz,) + packed.shape)
    wide = a2a(wide, ("gy", "gz")).reshape(cy, cz, *packed.shape)
    total_x = jnp.sum(wide[:, :, :nx], axis=(0, 1))
    total_y = jnp.sum(wide[:, :, nx : nx + ry], axis=1).reshape(cy * ry, C)
    total_z = jnp.sum(wide[:, :, nx + ry : nx + ry + rz], axis=0).reshape(cz * rz, C)
    packed = jnp.concatenate([total_x, total_y, total_z], axis=0)
    packed, got_value = lax.optimization_barrier((packed, got_value))
    pooled = a2a(jnp.broadcast_to(packed, (cx,) + packed.shape), "gx")

    part, q, kx = second(idx, pooled, w_qkv, keep, got_value, (nx, ny, nz))
    swap = [(0, 1), (1, 0)]
    gathered = a2a(part.reshape(cx * cy, nx, C), ("gx", "gy")).reshape(cx, cy, nx, C)
    spread = middle(gathered, kx).reshape(cx * cy, nx, C)
    mine = a2a(spread, ("gx", "gy")).reshape(part.shape)
    other = lax.ppermute(mine, "gz", swap)
    return third(idx, q, mine, other, tokens, w_out, w_gate_up, w_down)


def solution(mesh):
    in_specs = (P("gx", "gy", "gz", None), P(), P(), P(), P())
    out_specs = P("gx", "gy", "gz", None)
    return jax.shard_map(body, mesh=mesh, in_specs=in_specs, out_specs=out_specs, check_vma=False)
```

```python
import functools
import math

import jax
import jax.numpy as jnp
from jax import lax
from jax.experimental import pallas as pl
from jax.experimental.pallas import tpu as pltpu
from jax.sharding import PartitionSpec as P

HEADS = 8
HD = 16
C = 128
FF = 512
EPS = 1e-05

BF = jnp.bfloat16
F32 = jnp.float32
NT = (((1,), (1,)), ((), ()))


def dot(a, b, dims=(((1,), (0,)), ((), ()))):
    return lax.dot_general(a, b, dims, preferred_element_type=F32)


def dot(a, b, dims=(((1,), (0,)), ((), ()))):
    return lax.dot_general(a, b, dims, preferred_element_type=F32)


def norm_rows(values):
    mean = jnp.mean(values, axis=-1, keepdims=True)
    centred = values - mean
    spread = jnp.mean(centred * centred, axis=-1, keepdims=True)
    return centred * lax.rsqrt(spread + EPS)


def halves(values):
    high = values.astype(BF)
    low = (values - high.astype(F32)).astype(BF)
    return jnp.concatenate([high, low], axis=1)


def twice(values):
    return jnp.concatenate([values, values], axis=0)


def norm_rows_matmul(values):
    centred = values - jnp.mean(values, axis=-1, keepdims=True)
    mean_of = jnp.full((C, C), 1.0 / C, BF)
    spread = dot((centred * centred).astype(BF), mean_of)
    return centred * lax.rsqrt(spread + EPS)


def iota2(shape, dim):
    return lax.broadcasted_iota(jnp.int32, shape, dim)


def ones_where(cond):
    return jnp.where(cond, 1.0, 0.0).astype(BF)


def first_kernel(
    core_ref, tok_ref, wv_ref, keep_ref, send_ref, pool_ref, sx_ref, sy_acc, sz_acc
):
    step = pl.program_id(0)
    nb, ny, nz, _ = tok_ref.shape
    x = tok_ref[...].reshape(nb * ny * nz, C).astype(F32)
    normed = norm_rows_matmul(x).astype(BF)
    wvt = wv_ref[...].T
    turned = jnp.concatenate([wvt[C // 2 :], wvt[: C // 2]], axis=0)
    wvt = jnp.where(core_ref[0] == 0, wvt, turned)
    n32 = normed.astype(F32).reshape(nb, ny, nz, C)
    sxy = jnp.sum(n32, axis=2)
    sy = jnp.sum(sxy, axis=0)
    sz = jnp.sum(jnp.sum(n32, axis=0), axis=0)
    sx_ref[0] = jnp.sum(sxy, axis=1)
    for i in range(nb):
        vt = dot(wvt, normed[i * ny * nz : (i + 1) * ny * nz], NT).astype(BF)
        shape = (HEADS // 2, HD, ny * nz)
        keep_ref[:, i, :, :] = vt[: C // 2].reshape(shape)
        send_ref[:, i, :, :] = vt[C // 2 :].reshape(shape)

    @pl.when(step == 0)
    def _():
        sy_acc[...] = jnp.zeros_like(sy_acc)
        sz_acc[...] = jnp.zeros_like(sz_acc)

    sy_acc[...] += sy
    sz_acc[...] += sz

    @pl.when(step == pl.num_programs(0) - 1)
    def _():
        parts = pool_ref.shape[0]
        ry = ny // parts
        rz = nz // parts
        pool_ref[...] = jnp.zeros_like(pool_ref)
        pool_ref[:, 0:ry, :] = sy_acc[...].reshape(parts, ry, C)
        pool_ref[:, ry : ry + rz, :] = sz_acc[...].reshape(parts, rz, C)


def first(core, tokens, w_qkv, parts, block=4):
    nx, ny, nz, _ = tokens.shape
    rows = -(-(ny // parts + nz // parts) // 8) * 8
    half = HEADS // 2
    value = pl.BlockSpec((half, block, HD, ny * nz), lambda i, s: (0, i, 0, 0))
    return pl.pallas_call(
        first_kernel,
        grid_spec=pltpu.PrefetchScalarGridSpec(
            num_scalar_prefetch=1,
            grid=(nx // block,),
            in_specs=[
                pl.BlockSpec((block, ny, nz, C), lambda i, s: (i, 0, 0, 0)),
                pl.BlockSpec((C, C), lambda i, s: (0, 2)),
            ],
            out_specs=[
                value,
                value,
                pl.BlockSpec((parts, rows, C), lambda i, s: (0, 0, 0)),
                pl.BlockSpec((1, block, C), lambda i, s: (i, 0, 0)),
            ],
            scratch_shapes=[pltpu.VMEM((ny, C), F32), pltpu.VMEM((nz, C), F32)],
        ),
        out_shape=[
            jax.ShapeDtypeStruct((half, nx, HD, ny * nz), BF),
            jax.ShapeDtypeStruct((half, nx, HD, ny * nz), BF),
            jax.ShapeDtypeStruct((parts, rows, C), F32),
            jax.ShapeDtypeStruct((nx // block, block, C), F32),
        ],
        name="first",
    )(core, tokens, w_qkv)


def lane_expand(rows, first_head, heads, fine):
    shape = (C, heads * HD * HD)
    col = iota2(shape, 1)
    pick = (col % HD) if fine else (col % (HD * HD) // HD)
    channel = (first_head + col // (HD * HD)) * HD + pick
    return dot(halves(rows), twice(ones_where(iota2(shape, 0) == channel)))


def outer_yz(wide_y, wide_z, at):
    ny, nz = wide_y.shape[0], wide_z.shape[0]
    cut = slice(at * HD * HD, (at + 1) * HD * HD)
    both = wide_y[:, cut].reshape(ny, 1, HD * HD) * wide_z[:, cut].reshape(1, nz, HD * HD)
    return both.reshape(ny * nz, HD * HD).astype(BF)


def second_kernel(
    x_ref,
    y_ref,
    core_ref,
    r_ref,
    w_ref,
    mine_ref,
    got_ref,
    out_ref,
    qo_ref,
    kx_ref,
    k_scr,
    row_scr,
    *,
    sizes
):
    step = pl.program_id(0)
    nx, ny, nz = sizes
    px, rows, _ = r_ref.shape
    gx, gy, gz = x_ref[0], y_ref[0], core_ref[0]
    ry = ny // px
    rz = nz // px
    pz = 2
    py = (rows - nx - pz * rz) // ry
    half = HEADS // pz

    @pl.when(step == 0)
    def _():
        pooled = r_ref[...].reshape(px * rows, C)
        qk = dot(halves(pooled), twice(w_ref[...])).reshape(px, rows, 2 * C)
        cuts = (0, nx, nx + py * ry, rows)
        scaled = []
        for axis in range(3):
            part = qk[:, cuts[axis] : cuts[axis + 1], :]
            length = px * (cuts[axis + 1] - cuts[axis])
            total = jnp.sum(jnp.sum(part * part, axis=0), axis=0, keepdims=True)
            mean_q = jnp.sum(total[:, :C], axis=1, keepdims=True) / (length * C)
            mean_k = jnp.sum(total[:, C:], axis=1, keepdims=True) / (length * C)
            root = 1.0 / math.sqrt(HD * length)
            scaled.append((lax.rsqrt(mean_q + 1e-06) * root, lax.rsqrt(mean_k + 1e-06)))
        all_x = qk[:, 0:nx, :].reshape(px * nx, 2 * C)
        owned = gz * half + gx // (px // half)
        query = all_x[:, :C] * scaled[0][0]
        key_part = all_x[:, C:] * scaled[0][1]
        key_part = jnp.where(iota2(key_part.shape, 1) // HD == owned, key_part, 0.0)
        q_terms, k_terms = halves(query), halves(key_part)
        q_terms = jnp.concatenate([q_terms, q_terms[:, :C]], axis=1)
        k_terms = jnp.concatenate([k_terms[:, :C], k_terms[:, :C], k_terms[:, C:]], axis=1)
        kx_ref[...] = dot(q_terms, k_terms, NT).astype(BF)
        own_y = jnp.zeros((px, ry, 2 * C), F32)
        for g in range(py):
            at = nx + g * ry
            own_y = jnp.where(gy == g, qk[:, at : at + ry, :], own_y)
        own_y = own_y.reshape(ny, 2 * C)
        at = nx + py * ry
        low = qk[:, at : at + rz, :].reshape(nz, 2 * C)
        high = qk[:, at + rz : at + 2 * rz, :].reshape(nz, 2 * C)
        own_z = jnp.where(gz == 0, low, high)
        other_z = jnp.where(gz == 0, high, low)
        qo_ref[0:ny, :] = own_y[:, :C] * scaled[1][0]
        qo_ref[ny:, :] = own_z[:, :C] * scaled[2][0]
        k_scr[0:ny, :] = own_y[:, C:] * scaled[1][1]
        k_scr[ny : ny + nz, :] = own_z[:, C:] * scaled[2][1]
        k_scr[ny + nz :, :] = other_z[:, C:] * scaled[2][1]

    heads = mine_ref.shape[0]
    first_head = gz * half + step * heads
    wide_y = lane_expand(k_scr[0:ny, :], first_head, heads, False)
    wide_z = lane_expand(k_scr[ny:, :], first_head, heads, True)
    for j in range(heads):
        narrow = jnp.zeros((nx * HD, HD * HD), F32)
        for i, source in enumerate((mine_ref, got_ref)):
            mixer = outer_yz(wide_y, wide_z[i * nz : (i + 1) * nz], j)
            narrow = narrow + dot(source[j].reshape(nx * HD, ny * nz), mixer)
        for side in range(2):
            row_scr[j, side] = narrow[:, side * C : (side + 1) * C]
            for channel in range(HD):
                rows = row_scr[j, side, pl.ds(channel, nx, stride=HD), :]
                out_ref[j * HD + channel, side] = rows.astype(BF)


def second(where, pooled, w_qkv, mine, got, sizes, steps=1):
    nx, ny, nz = sizes
    half = HEADS // 2
    heads = half // steps
    value = pl.BlockSpec((heads, nx, HD, ny * nz), lambda i, *s: (i, 0, 0, 0))
    return pl.pallas_call(
        functools.partial(second_kernel, sizes=sizes),
        grid_spec=pltpu.PrefetchScalarGridSpec(
            num_scalar_prefetch=len(where),
            grid=(steps,),
            in_specs=[
                pl.BlockSpec(memory_space=pltpu.VMEM),
                pl.BlockSpec((C, 2 * C), lambda i, *s: (0, 0)),
                value,
                value,
            ],
            out_specs=[
                pl.BlockSpec((heads * HD, 2, nx, C), lambda i, *s: (i, 0, 0, 0)),
                pl.BlockSpec((ny + nz, C), lambda i, *s: (0, 0)),
                pl.BlockSpec((C, C), lambda i, *s: (0, 0)),
            ],
            scratch_shapes=[
                pltpu.VMEM((ny + 2 * nz, C), F32),
                pltpu.VMEM((heads, 2, nx * HD, C), F32),
            ],
        ),
        out_shape=[
            jax.ShapeDtypeStruct((half * HD, 2, nx, C), BF),
            jax.ShapeDtypeStruct((ny + nz, C), F32),
            jax.ShapeDtypeStruct((C, C), BF),
        ],
        name="second",
    )(*where, pooled, w_qkv, mine, got)


def middle_kernel(g_ref, kx_ref, out_ref):
    px, py, nx, _ = g_ref.shape
    lines = jnp.sum(g_ref[...].astype(F32), axis=1).reshape(px * nx, C)
    high = lines.astype(BF)
    low = (lines - high.astype(F32)).astype(BF)
    kx = kx_ref[...]
    mixed = dot(jnp.concatenate([kx, kx], axis=1), jnp.concatenate([high, low], axis=0))
    mixed = mixed.astype(BF).reshape(px, 1, nx, C)
    out_ref[...] = jnp.broadcast_to(mixed, out_ref.shape)


def middle(gathered, kx):
    vmem = pl.BlockSpec(memory_space=pltpu.VMEM)
    return pl.pallas_call(
        middle_kernel,
        in_specs=[vmem, vmem],
        out_specs=vmem,
        out_shape=jax.ShapeDtypeStruct(gathered.shape, BF),
        name="middle",
    )(gathered, kx)


def third_kernel(
    core_ref, q_ref, mine_ref, other_ref, tok_ref, wo_ref, wg_ref, wd_ref, out_ref, mix_scr, row_scr
):
    step = pl.program_id(0)
    nb, ny, nz, _ = tok_ref.shape
    nx = mix_scr.shape[0]
    half = HEADS // 2
    gz = core_ref[0]

    @pl.when(step == 0)
    def _():
        qy = q_ref[0:ny, :]
        qz = q_ref[ny : ny + nz, :]
        wides = []
        for head in (gz * half, (1 - gz) * half):
            wide_y = lane_expand(qy, head, half, False)
            wides.append((wide_y, lane_expand(qz, head, half, True)))
        for j in range(HEADS):
            source = mine_ref if j < half else other_ref
            head = jnp.where(gz == 0, j, (j + half) % HEADS)
            at = j % half * HD
            mixer = outer_yz(*wides[j // half], j % half)
            for i in range(2):
                rows = source[at : at + HD, i].astype(F32).reshape(HD * nx, C)
                row_scr[j, i] = rows
            narrow = jnp.concatenate(
                [
                    jnp.concatenate(
                        [row_scr[j, i, pl.ds(k, HD, stride=nx), :] for k in range(nx)], axis=0
                    )
                    for i in range(2)
                ],
                axis=1,
            ).astype(BF)
            mixed = dot(narrow, mixer, NT).astype(BF)
            mix_scr[:, head, :, :] = mixed.reshape(nx, HD, ny * nz)

    mixed = [mix_scr[step * nb + i].reshape(C, ny * nz).T for i in range(nb)]
    mixed = jnp.concatenate(mixed, axis=0)
    tok = tok_ref[...].reshape(nb * ny * nz, C)
    resid = tok.astype(F32) + dot(mixed, wo_ref[...])
    inner = norm_rows_matmul(resid).astype(BF)
    both = dot(inner, wg_ref[...]).astype(BF)
    gate = both[:, :FF]
    root = math.sqrt(2.0 / math.pi)
    inside = gate * (BF(root) + BF(root * 0.044715) * (gate * gate))
    half_gate = gate * BF(0.5)
    hidden = (half_gate + half_gate * jnp.tanh(inside)) * both[:, FF:]
    result = (resid + dot(hidden, wd_ref[...])).astype(BF)
    out_ref[...] = result.reshape(nb, ny, nz, C)


def third(core, q, mine, other, tokens, w_out, w_gate_up, w_down, block=2):
    nx, ny, nz, _ = tokens.shape
    full = lambda a: pl.BlockSpec(a.shape, lambda i, s: (0,) * a.ndim)
    slab = pl.BlockSpec((block, ny, nz, C), lambda i, s: (i, 0, 0, 0))
    vmem = pl.BlockSpec(memory_space=pltpu.VMEM)
    return pl.pallas_call(
        third_kernel,
        grid_spec=pltpu.PrefetchScalarGridSpec(
            num_scalar_prefetch=1,
            grid=(nx // block,),
            in_specs=[
                full(q),
                vmem,
                vmem,
                slab,
                full(w_out),
                full(w_gate_up),
                full(w_down),
            ],
            out_specs=slab,
            scratch_shapes=[
                pltpu.VMEM((nx, HEADS, HD, ny * nz), BF),
                pltpu.VMEM((HEADS, 2, nx * HD, C), F32),
            ],
        ),
        out_shape=jax.ShapeDtypeStruct(tokens.shape, BF),
        name="third",
    )(core, q, mine, other, tokens, w_out, w_gate_up, w_down)


def a2a(values, axes):
    return lax.all_to_all(values, axes, 0, 0, tiled=True)


def body(tokens, w_qkv, w_out, w_gate_up, w_down):
    nx, ny, nz, _ = tokens.shape
    cx, cy, cz = (lax.axis_size(a) for a in ("gx", "gy", "gz"))
    where = [lax.axis_index(a).astype(jnp.int32).reshape(1) for a in ("gx", "gy", "gz")]
    ry = ny // cx
    rz = nz // cx
    keep, send, pool, sum_x = first(where[2], tokens, w_qkv, cx)
    got_value = lax.ppermute(send, "gz", [(0, 1), (1, 0)])
    sum_x = sum_x.reshape(nx, C)
    pool, where = lax.optimization_barrier((pool, where))
    got = jnp.sum(a2a(pool, "gx"), axis=0)
    packed = jnp.concatenate([sum_x, got], axis=0)
    wide = jnp.broadcast_to(packed, (cy * cz,) + packed.shape)
    wide = a2a(wide, ("gy", "gz")).reshape(cy, cz, *packed.shape)
    total_x = jnp.sum(wide[:, :, :nx], axis=(0, 1))
    total_y = jnp.sum(wide[:, :, nx : nx + ry], axis=1).reshape(cy * ry, C)
    total_z = jnp.sum(wide[:, :, nx + ry : nx + ry + rz], axis=0).reshape(cz * rz, C)
    packed = jnp.concatenate([total_x, total_y, total_z], axis=0)
    packed, got_value = lax.optimization_barrier((packed, got_value))
    pooled = a2a(jnp.broadcast_to(packed, (cx,) + packed.shape), "gx")

    part, q, kx = second(where, pooled, w_qkv, keep, got_value, (nx, ny, nz))
    swap = [(0, 1), (1, 0)]
    gathered = a2a(part.reshape(cx * cy, nx, C), ("gx", "gy")).reshape(cx, cy, nx, C)
    spread = middle(gathered, kx).reshape(cx * cy, nx, C)
    mine = a2a(spread, ("gx", "gy")).reshape(part.shape)
    other = lax.ppermute(mine, "gz", swap)
    return third(where[2], q, mine, other, tokens, w_out, w_gate_up, w_down)


def solution(mesh):
    in_specs = (P("gx", "gy", "gz", None), P(), P(), P(), P())
    out_specs = P("gx", "gy", "gz", None)
    return jax.shard_map(body, mesh=mesh, in_specs=in_specs, out_specs=out_specs, check_vma=False)
```

```python
import functools
import math

import jax
import jax.numpy as jnp
from jax import lax
from jax.experimental import pallas as pl
from jax.experimental.pallas import tpu as pltpu
from jax.sharding import PartitionSpec as P

HEADS = 8
HD = 16
C = 128
FF = 512
EPS = 1e-05

BF = jnp.bfloat16
F32 = jnp.float32
NT = (((1,), (1,)), ((), ()))


def dot(a, b, dims=(((1,), (0,)), ((), ()))):
    return lax.dot_general(a, b, dims, preferred_element_type=F32)


def dot(a, b, dims=(((1,), (0,)), ((), ()))):
    return lax.dot_general(a, b, dims, preferred_element_type=F32)


def norm_rows(values):
    mean = jnp.mean(values, axis=-1, keepdims=True)
    centred = values - mean
    spread = jnp.mean(centred * centred, axis=-1, keepdims=True)
    return centred * lax.rsqrt(spread + EPS)


def halves(values):
    high = values.astype(BF)
    low = (values - high.astype(F32)).astype(BF)
    return jnp.concatenate([high, low], axis=1)


def twice(values):
    return jnp.concatenate([values, values], axis=0)


def norm_rows_matmul(values):
    centred = values - jnp.mean(values, axis=-1, keepdims=True)
    mean_of = jnp.full((C, C), 1.0 / C, BF)
    spread = dot((centred * centred).astype(BF), mean_of)
    return centred * lax.rsqrt(spread + EPS)


def iota2(shape, dim):
    return lax.broadcasted_iota(jnp.int32, shape, dim)


def ones_where(cond):
    return jnp.where(cond, 1.0, 0.0).astype(BF)


def first_kernel(
    core_ref, tok_ref, wv_ref, keep_ref, send_ref, pool_ref, sx_ref, sy_acc, sz_acc
):
    step = pl.program_id(0)
    nb, ny, nz, _ = tok_ref.shape
    x = tok_ref[...].reshape(nb * ny * nz, C).astype(F32)
    normed = norm_rows_matmul(x).astype(BF)
    wvt = wv_ref[...].T
    turned = jnp.concatenate([wvt[C // 2 :], wvt[: C // 2]], axis=0)
    wvt = jnp.where(core_ref[0] == 0, wvt, turned)
    n32 = normed.astype(F32).reshape(nb, ny, nz, C)
    sxy = jnp.sum(n32, axis=2)
    sy = jnp.sum(sxy, axis=0)
    sz = jnp.sum(jnp.sum(n32, axis=0), axis=0)
    sx_ref[0] = jnp.sum(sxy, axis=1)
    for i in range(nb):
        vt = dot(wvt, normed[i * ny * nz : (i + 1) * ny * nz], NT).astype(BF)
        shape = (HEADS // 2, HD, ny * nz)
        keep_ref[:, i, :, :] = vt[: C // 2].reshape(shape)
        send_ref[:, i, :, :] = vt[C // 2 :].reshape(shape)

    @pl.when(step == 0)
    def _():
        sy_acc[...] = jnp.zeros_like(sy_acc)
        sz_acc[...] = jnp.zeros_like(sz_acc)

    sy_acc[...] += sy
    sz_acc[...] += sz

    @pl.when(step == pl.num_programs(0) - 1)
    def _():
        parts = pool_ref.shape[0]
        ry = ny // parts
        rz = nz // parts
        pool_ref[...] = jnp.zeros_like(pool_ref)
        pool_ref[:, 0:ry, :] = sy_acc[...].reshape(parts, ry, C)
        pool_ref[:, ry : ry + rz, :] = sz_acc[...].reshape(parts, rz, C)


def first(core, tokens, w_qkv, parts, block=4):
    nx, ny, nz, _ = tokens.shape
    rows = -(-(ny // parts + nz // parts) // 8) * 8
    half = HEADS // 2
    value = pl.BlockSpec((half, block, HD, ny * nz), lambda i, s: (0, i, 0, 0))
    return pl.pallas_call(
        first_kernel,
        grid_spec=pltpu.PrefetchScalarGridSpec(
            num_scalar_prefetch=1,
            grid=(nx // block,),
            in_specs=[
                pl.BlockSpec((block, ny, nz, C), lambda i, s: (i, 0, 0, 0)),
                pl.BlockSpec((C, C), lambda i, s: (0, 2)),
            ],
            out_specs=[
                value,
                value,
                pl.BlockSpec((parts, rows, C), lambda i, s: (0, 0, 0)),
                pl.BlockSpec((1, block, C), lambda i, s: (i, 0, 0)),
            ],
            scratch_shapes=[pltpu.VMEM((ny, C), F32), pltpu.VMEM((nz, C), F32)],
        ),
        out_shape=[
            jax.ShapeDtypeStruct((half, nx, HD, ny * nz), BF),
            jax.ShapeDtypeStruct((half, nx, HD, ny * nz), BF),
            jax.ShapeDtypeStruct((parts, rows, C), F32),
            jax.ShapeDtypeStruct((nx // block, block, C), F32),
        ],
        name="first",
    )(core, tokens, w_qkv)


def lane_expand(rows, first_head, heads, fine):
    shape = (C, heads * HD * HD)
    col = iota2(shape, 1)
    pick = (col % HD) if fine else (col % (HD * HD) // HD)
    channel = (first_head + col // (HD * HD)) * HD + pick
    return dot(halves(rows), twice(ones_where(iota2(shape, 0) == channel)))


def outer_yz(wide_y, wide_z, at):
    ny, nz = wide_y.shape[0], wide_z.shape[0]
    cut = slice(at * HD * HD, (at + 1) * HD * HD)
    both = wide_y[:, cut].reshape(ny, 1, HD * HD) * wide_z[:, cut].reshape(1, nz, HD * HD)
    return both.reshape(ny * nz, HD * HD).astype(BF)


def second_kernel(
    x_ref,
    y_ref,
    core_ref,
    r_ref,
    w_ref,
    mine_ref,
    got_ref,
    out_ref,
    qo_ref,
    kx_ref,
    k_scr,
    row_scr,
    *,
    sizes
):
    step = pl.program_id(0)
    nx, ny, nz = sizes
    px, rows, _ = r_ref.shape
    gx, gy, gz = x_ref[0], y_ref[0], core_ref[0]
    ry = ny // px
    rz = nz // px
    pz = 2
    py = (rows - nx - pz * rz) // ry
    half = HEADS // pz

    @pl.when(step == 0)
    def _():
        pooled = r_ref[...].reshape(px * rows, C)
        qk = dot(halves(pooled), twice(w_ref[...])).reshape(px, rows, 2 * C)
        cuts = (0, nx, nx + py * ry, rows)
        scaled = []
        for axis in range(3):
            part = qk[:, cuts[axis] : cuts[axis + 1], :]
            length = px * (cuts[axis + 1] - cuts[axis])
            total = jnp.sum(jnp.sum(part * part, axis=0), axis=0, keepdims=True)
            mean_q = jnp.sum(total[:, :C], axis=1, keepdims=True) / (length * C)
            mean_k = jnp.sum(total[:, C:], axis=1, keepdims=True) / (length * C)
            root = 1.0 / math.sqrt(HD * length)
            scaled.append((lax.rsqrt(mean_q + 1e-06) * root, lax.rsqrt(mean_k + 1e-06)))
        all_x = qk[:, 0:nx, :].reshape(px * nx, 2 * C)
        owned = gz * half + gx // (px // half)
        query = all_x[:, :C] * scaled[0][0]
        key_part = all_x[:, C:] * scaled[0][1]
        key_part = jnp.where(iota2(key_part.shape, 1) // HD == owned, key_part, 0.0)
        q_terms, k_terms = halves(query), halves(key_part)
        q_terms = jnp.concatenate([q_terms, q_terms[:, :C]], axis=1)
        k_terms = jnp.concatenate([k_terms[:, :C], k_terms[:, :C], k_terms[:, C:]], axis=1)
        kx_ref[...] = dot(q_terms, k_terms, NT).astype(BF)
        own_y = jnp.zeros((px, ry, 2 * C), F32)
        for g in range(py):
            at = nx + g * ry
            own_y = jnp.where(gy == g, qk[:, at : at + ry, :], own_y)
        own_y = own_y.reshape(ny, 2 * C)
        at = nx + py * ry
        low = qk[:, at : at + rz, :].reshape(nz, 2 * C)
        high = qk[:, at + rz : at + 2 * rz, :].reshape(nz, 2 * C)
        own_z = jnp.where(gz == 0, low, high)
        other_z = jnp.where(gz == 0, high, low)
        qo_ref[0:ny, :] = own_y[:, :C] * scaled[1][0]
        qo_ref[ny:, :] = own_z[:, :C] * scaled[2][0]
        k_scr[0:ny, :] = own_y[:, C:] * scaled[1][1]
        k_scr[ny : ny + nz, :] = own_z[:, C:] * scaled[2][1]
        k_scr[ny + nz :, :] = other_z[:, C:] * scaled[2][1]

    heads = mine_ref.shape[0]
    first_head = gz * half + step * heads
    wide_y = lane_expand(k_scr[0:ny, :], first_head, heads, False)
    wide_z = lane_expand(k_scr[ny:, :], first_head, heads, True)
    for j in range(heads):
        narrow = jnp.zeros((nx * HD, HD * HD), F32)
        for i, source in enumerate((mine_ref, got_ref)):
            mixer = outer_yz(wide_y, wide_z[i * nz : (i + 1) * nz], j)
            narrow = narrow + dot(source[j].reshape(nx * HD, ny * nz), mixer)
        for side in range(2):
            row_scr[j, side] = narrow[:, side * C : (side + 1) * C]
            for channel in range(HD):
                rows = row_scr[j, side, pl.ds(channel, nx, stride=HD), :]
                out_ref[j * HD + channel, side] = rows.astype(BF)


def second(where, pooled, w_qkv, mine, got, sizes, steps=1):
    nx, ny, nz = sizes
    half = HEADS // 2
    heads = half // steps
    value = pl.BlockSpec((heads, nx, HD, ny * nz), lambda i, *s: (i, 0, 0, 0))
    return pl.pallas_call(
        functools.partial(second_kernel, sizes=sizes),
        grid_spec=pltpu.PrefetchScalarGridSpec(
            num_scalar_prefetch=len(where),
            grid=(steps,),
            in_specs=[
                pl.BlockSpec(memory_space=pltpu.VMEM),
                pl.BlockSpec((C, 2 * C), lambda i, *s: (0, 0)),
                value,
                value,
            ],
            out_specs=[
                pl.BlockSpec((heads * HD, 2, nx, C), lambda i, *s: (i, 0, 0, 0)),
                pl.BlockSpec((ny + nz, C), lambda i, *s: (0, 0)),
                pl.BlockSpec((C, C), lambda i, *s: (0, 0)),
            ],
            scratch_shapes=[
                pltpu.VMEM((ny + 2 * nz, C), F32),
                pltpu.VMEM((heads, 2, nx * HD, C), F32),
            ],
        ),
        out_shape=[
            jax.ShapeDtypeStruct((half * HD, 2, nx, C), BF),
            jax.ShapeDtypeStruct((ny + nz, C), F32),
            jax.ShapeDtypeStruct((C, C), BF),
        ],
        name="second",
    )(*where, pooled, w_qkv, mine, got)


def middle_kernel(g_ref, kx_ref, out_ref):
    px, py, nx, _ = g_ref.shape
    lines = jnp.sum(g_ref[...].astype(F32), axis=1).reshape(px * nx, C)
    high = lines.astype(BF)
    low = (lines - high.astype(F32)).astype(BF)
    kx = kx_ref[...]
    mixed = dot(jnp.concatenate([kx, kx], axis=1), jnp.concatenate([high, low], axis=0))
    mixed = mixed.astype(BF).reshape(px, 1, nx, C)
    out_ref[...] = jnp.broadcast_to(mixed, out_ref.shape)


def middle(gathered, kx):
    vmem = pl.BlockSpec(memory_space=pltpu.VMEM)
    return pl.pallas_call(
        middle_kernel,
        in_specs=[vmem, vmem],
        out_specs=vmem,
        out_shape=jax.ShapeDtypeStruct(gathered.shape, BF),
        name="middle",
    )(gathered, kx)


def third_kernel(
    core_ref, q_ref, mine_ref, other_ref, tok_ref, wo_ref, wg_ref, wd_ref, out_ref, mix_scr, row_scr
):
    step = pl.program_id(0)
    nb, ny, nz, _ = tok_ref.shape
    nx = mix_scr.shape[0]
    half = HEADS // 2
    gz = core_ref[0]

    @pl.when(step == 0)
    def _():
        qy = q_ref[0:ny, :]
        qz = q_ref[ny : ny + nz, :]
        wides = []
        for head in (gz * half, (1 - gz) * half):
            wide_y = lane_expand(qy, head, half, False)
            wides.append((wide_y, lane_expand(qz, head, half, True)))
        for j in range(HEADS):
            source = mine_ref if j < half else other_ref
            head = jnp.where(gz == 0, j, (j + half) % HEADS)
            at = j % half * HD
            mixer = outer_yz(*wides[j // half], j % half)
            for i in range(2):
                rows = source[at : at + HD, i].astype(F32).reshape(HD * nx, C)
                row_scr[j, i] = rows
            narrow = jnp.concatenate(
                [
                    jnp.concatenate(
                        [row_scr[j, i, pl.ds(k, HD, stride=nx), :] for k in range(nx)], axis=0
                    )
                    for i in range(2)
                ],
                axis=1,
            ).astype(BF)
            mixed = dot(narrow, mixer, NT).astype(BF)
            mix_scr[:, head, :, :] = mixed.reshape(nx, HD, ny * nz)

    mixed = [mix_scr[step * nb + i].reshape(C, ny * nz).T for i in range(nb)]
    mixed = jnp.concatenate(mixed, axis=0)
    tok = tok_ref[...].reshape(nb * ny * nz, C)
    resid = tok.astype(F32) + dot(mixed, wo_ref[...])
    inner = norm_rows_matmul(resid).astype(BF)
    both = dot(inner, wg_ref[...]).astype(BF)
    gate = both[:, :FF]
    root = math.sqrt(2.0 / math.pi)
    inside = gate * (BF(2 * root) + BF(2 * root * 0.044715) * (gate * gate))
    hidden = gate * jax.nn.sigmoid(inside) * both[:, FF:]
    result = (resid + dot(hidden, wd_ref[...])).astype(BF)
    out_ref[...] = result.reshape(nb, ny, nz, C)


def third(core, q, mine, other, tokens, w_out, w_gate_up, w_down, block=2):
    nx, ny, nz, _ = tokens.shape
    full = lambda a: pl.BlockSpec(a.shape, lambda i, s: (0,) * a.ndim)
    slab = pl.BlockSpec((block, ny, nz, C), lambda i, s: (i, 0, 0, 0))
    vmem = pl.BlockSpec(memory_space=pltpu.VMEM)
    return pl.pallas_call(
        third_kernel,
        grid_spec=pltpu.PrefetchScalarGridSpec(
            num_scalar_prefetch=1,
            grid=(nx // block,),
            in_specs=[
                full(q),
                vmem,
                vmem,
                slab,
                full(w_out),
                full(w_gate_up),
                full(w_down),
            ],
            out_specs=slab,
            scratch_shapes=[
                pltpu.VMEM((nx, HEADS, HD, ny * nz), BF),
                pltpu.VMEM((HEADS, 2, nx * HD, C), F32),
            ],
        ),
        out_shape=jax.ShapeDtypeStruct(tokens.shape, BF),
        name="third",
    )(core, q, mine, other, tokens, w_out, w_gate_up, w_down)


def a2a(values, axes):
    return lax.all_to_all(values, axes, 0, 0, tiled=True)


def body(tokens, w_qkv, w_out, w_gate_up, w_down):
    nx, ny, nz, _ = tokens.shape
    cx, cy, cz = (lax.axis_size(a) for a in ("gx", "gy", "gz"))
    where = [lax.axis_index(a).astype(jnp.int32).reshape(1) for a in ("gx", "gy", "gz")]
    ry = ny // cx
    rz = nz // cx
    keep, send, pool, sum_x = first(where[2], tokens, w_qkv, cx)
    got_value = lax.ppermute(send, "gz", [(0, 1), (1, 0)])
    sum_x = sum_x.reshape(nx, C)
    pool, where = lax.optimization_barrier((pool, where))
    got = jnp.sum(a2a(pool, "gx"), axis=0)
    packed = jnp.concatenate([sum_x, got], axis=0)
    wide = jnp.broadcast_to(packed, (cy * cz,) + packed.shape)
    wide = a2a(wide, ("gy", "gz")).reshape(cy, cz, *packed.shape)
    total_x = jnp.sum(wide[:, :, :nx], axis=(0, 1))
    total_y = jnp.sum(wide[:, :, nx : nx + ry], axis=1).reshape(cy * ry, C)
    total_z = jnp.sum(wide[:, :, nx + ry : nx + ry + rz], axis=0).reshape(cz * rz, C)
    packed = jnp.concatenate([total_x, total_y, total_z], axis=0)
    packed, got_value = lax.optimization_barrier((packed, got_value))
    pooled = a2a(jnp.broadcast_to(packed, (cx,) + packed.shape), "gx")

    part, q, kx = second(where, pooled, w_qkv, keep, got_value, (nx, ny, nz))
    swap = [(0, 1), (1, 0)]
    gathered = a2a(part.reshape(cx * cy, nx, C), ("gx", "gy")).reshape(cx, cy, nx, C)
    spread = middle(gathered, kx).reshape(cx * cy, nx, C)
    mine = a2a(spread, ("gx", "gy")).reshape(part.shape)
    other = lax.ppermute(mine, "gz", swap)
    return third(where[2], q, mine, other, tokens, w_out, w_gate_up, w_down)


def solution(mesh):
    in_specs = (P("gx", "gy", "gz", None), P(), P(), P(), P())
    out_specs = P("gx", "gy", "gz", None)
    return jax.shard_map(body, mesh=mesh, in_specs=in_specs, out_specs=out_specs, check_vma=False)
```

```python
import functools
import math

import jax
import jax.numpy as jnp
from jax import lax
from jax.experimental import pallas as pl
from jax.experimental.pallas import tpu as pltpu
from jax.sharding import PartitionSpec as P

HEADS = 8
HD = 16
C = 128
FF = 512
EPS = 1e-05

BF = jnp.bfloat16
F32 = jnp.float32
NT = (((1,), (1,)), ((), ()))


def dot(a, b, dims=(((1,), (0,)), ((), ()))):
    return lax.dot_general(a, b, dims, preferred_element_type=F32)


def dot(a, b, dims=(((1,), (0,)), ((), ()))):
    return lax.dot_general(a, b, dims, preferred_element_type=F32)


def norm_rows(values):
    mean = jnp.mean(values, axis=-1, keepdims=True)
    centred = values - mean
    spread = jnp.mean(centred * centred, axis=-1, keepdims=True)
    return centred * lax.rsqrt(spread + EPS)


def halves(values):
    high = values.astype(BF)
    low = (values - high.astype(F32)).astype(BF)
    return jnp.concatenate([high, low], axis=1)


def twice(values):
    return jnp.concatenate([values, values], axis=0)


def norm_rows_matmul(values):
    centred = values - jnp.mean(values, axis=-1, keepdims=True)
    mean_of = jnp.full((C, C), 1.0 / C, BF)
    spread = dot((centred * centred).astype(BF), mean_of)
    return centred * lax.rsqrt(spread + EPS)


def iota2(shape, dim):
    return lax.broadcasted_iota(jnp.int32, shape, dim)


def ones_where(cond):
    return jnp.where(cond, 1.0, 0.0).astype(BF)


def first_kernel(
    core_ref, tok_ref, wv_ref, keep_ref, send_ref, pool_ref, sx_ref, sy_acc, sz_acc
):
    step = pl.program_id(0)
    nb, ny, nz, _ = tok_ref.shape
    x = tok_ref[...].reshape(nb * ny * nz, C).astype(F32)
    normed = norm_rows_matmul(x).astype(BF)
    wvt = wv_ref[...].T
    turned = jnp.concatenate([wvt[C // 2 :], wvt[: C // 2]], axis=0)
    wvt = jnp.where(core_ref[0] == 0, wvt, turned)
    n32 = normed.astype(F32).reshape(nb, ny, nz, C)
    sxy = jnp.sum(n32, axis=2)
    sy = jnp.sum(sxy, axis=0)
    sz = jnp.sum(jnp.sum(n32, axis=0), axis=0)
    sx_ref[0] = jnp.sum(sxy, axis=1)
    for i in range(nb):
        vt = dot(wvt, normed[i * ny * nz : (i + 1) * ny * nz], NT).astype(BF)
        shape = (HEADS // 2, HD, ny * nz)
        keep_ref[:, i, :, :] = vt[: C // 2].reshape(shape)
        send_ref[:, i, :, :] = vt[C // 2 :].reshape(shape)

    @pl.when(step == 0)
    def _():
        sy_acc[...] = jnp.zeros_like(sy_acc)
        sz_acc[...] = jnp.zeros_like(sz_acc)

    sy_acc[...] += sy
    sz_acc[...] += sz

    @pl.when(step == pl.num_programs(0) - 1)
    def _():
        parts = pool_ref.shape[0]
        ry = ny // parts
        rz = nz // parts
        pool_ref[...] = jnp.zeros_like(pool_ref)
        pool_ref[:, 0:ry, :] = sy_acc[...].reshape(parts, ry, C)
        pool_ref[:, ry : ry + rz, :] = sz_acc[...].reshape(parts, rz, C)


def first(core, tokens, w_qkv, parts, block=4):
    nx, ny, nz, _ = tokens.shape
    rows = -(-(ny // parts + nz // parts) // 8) * 8
    half = HEADS // 2
    value = pl.BlockSpec((half, block, HD, ny * nz), lambda i, s: (0, i, 0, 0))
    return pl.pallas_call(
        first_kernel,
        grid_spec=pltpu.PrefetchScalarGridSpec(
            num_scalar_prefetch=1,
            grid=(nx // block,),
            in_specs=[
                pl.BlockSpec((block, ny, nz, C), lambda i, s: (i, 0, 0, 0)),
                pl.BlockSpec((C, C), lambda i, s: (0, 2)),
            ],
            out_specs=[
                value,
                value,
                pl.BlockSpec((parts, rows, C), lambda i, s: (0, 0, 0)),
                pl.BlockSpec((1, block, C), lambda i, s: (i, 0, 0)),
            ],
            scratch_shapes=[pltpu.VMEM((ny, C), F32), pltpu.VMEM((nz, C), F32)],
        ),
        out_shape=[
            jax.ShapeDtypeStruct((half, nx, HD, ny * nz), BF),
            jax.ShapeDtypeStruct((half, nx, HD, ny * nz), BF),
            jax.ShapeDtypeStruct((parts, rows, C), F32),
            jax.ShapeDtypeStruct((nx // block, block, C), F32),
        ],
        name="first",
    )(core, tokens, w_qkv)


def lane_expand(rows, first_head, heads, fine):
    shape = (C, heads * HD * HD)
    col = iota2(shape, 1)
    pick = (col % HD) if fine else (col % (HD * HD) // HD)
    channel = (first_head + col // (HD * HD)) * HD + pick
    return dot(halves(rows), twice(ones_where(iota2(shape, 0) == channel)))


def outer_yz(wide_y, wide_z, at, narrow=False):
    ny, nz = wide_y.shape[0], wide_z.shape[0]
    cut = slice(at * HD * HD, (at + 1) * HD * HD)
    wide_y = wide_y[:, cut].reshape(ny, 1, HD * HD)
    wide_z = wide_z[:, cut].reshape(1, nz, HD * HD)
    if narrow:
        wide_y = jnp.broadcast_to(wide_y.astype(BF), (ny, nz, HD * HD))
        wide_z = wide_z.astype(BF)
    return (wide_y * wide_z).reshape(ny * nz, HD * HD).astype(BF)


def second_kernel(
    x_ref,
    y_ref,
    core_ref,
    r_ref,
    w_ref,
    mine_ref,
    got_ref,
    out_ref,
    qo_ref,
    kx_ref,
    k_scr,
    row_scr,
    *,
    sizes
):
    step = pl.program_id(0)
    nx, ny, nz = sizes
    px, rows, _ = r_ref.shape
    gx, gy, gz = x_ref[0], y_ref[0], core_ref[0]
    ry = ny // px
    rz = nz // px
    pz = 2
    py = (rows - nx - pz * rz) // ry
    half = HEADS // pz

    @pl.when(step == 0)
    def _():
        pooled = r_ref[...].reshape(px * rows, C)
        qk = dot(halves(pooled), twice(w_ref[...])).reshape(px, rows, 2 * C)
        cuts = (0, nx, nx + py * ry, rows)
        scaled = []
        for axis in range(3):
            part = qk[:, cuts[axis] : cuts[axis + 1], :]
            length = px * (cuts[axis + 1] - cuts[axis])
            total = jnp.sum(jnp.sum(part * part, axis=0), axis=0, keepdims=True)
            mean_q = jnp.sum(total[:, :C], axis=1, keepdims=True) / (length * C)
            mean_k = jnp.sum(total[:, C:], axis=1, keepdims=True) / (length * C)
            root = 1.0 / math.sqrt(HD * length)
            scaled.append((lax.rsqrt(mean_q + 1e-06) * root, lax.rsqrt(mean_k + 1e-06)))
        all_x = qk[:, 0:nx, :].reshape(px * nx, 2 * C)
        owned = gz * half + gx // (px // half)
        query = all_x[:, :C] * scaled[0][0]
        key_part = all_x[:, C:] * scaled[0][1]
        key_part = jnp.where(iota2(key_part.shape, 1) // HD == owned, key_part, 0.0)
        q_terms, k_terms = halves(query), halves(key_part)
        q_terms = jnp.concatenate([q_terms, q_terms[:, :C]], axis=1)
        k_terms = jnp.concatenate([k_terms[:, :C], k_terms[:, :C], k_terms[:, C:]], axis=1)
        kx_ref[...] = dot(q_terms, k_terms, NT).astype(BF)
        own_y = jnp.zeros((px, ry, 2 * C), F32)
        for g in range(py):
            at = nx + g * ry
            own_y = jnp.where(gy == g, qk[:, at : at + ry, :], own_y)
        own_y = own_y.reshape(ny, 2 * C)
        at = nx + py * ry
        low = qk[:, at : at + rz, :].reshape(nz, 2 * C)
        high = qk[:, at + rz : at + 2 * rz, :].reshape(nz, 2 * C)
        own_z = jnp.where(gz == 0, low, high)
        other_z = jnp.where(gz == 0, high, low)
        qo_ref[0:ny, :] = own_y[:, :C] * scaled[1][0]
        qo_ref[ny:, :] = own_z[:, :C] * scaled[2][0]
        k_scr[0:ny, :] = own_y[:, C:] * scaled[1][1]
        k_scr[ny : ny + nz, :] = own_z[:, C:] * scaled[2][1]
        k_scr[ny + nz :, :] = other_z[:, C:] * scaled[2][1]

    heads = mine_ref.shape[0]
    first_head = gz * half + step * heads
    wide_y = lane_expand(k_scr[0:ny, :], first_head, heads, False)
    wide_z = lane_expand(k_scr[ny:, :], first_head, heads, True)
    for j in range(heads):
        narrow = jnp.zeros((nx * HD, HD * HD), F32)
        for i, source in enumerate((mine_ref, got_ref)):
            mixer = outer_yz(wide_y, wide_z[i * nz : (i + 1) * nz], j, narrow=True)
            narrow = narrow + dot(source[j].reshape(nx * HD, ny * nz), mixer)
        for side in range(2):
            row_scr[j, side] = narrow[:, side * C : (side + 1) * C]
            for channel in range(HD):
                rows = row_scr[j, side, pl.ds(channel, nx, stride=HD), :]
                out_ref[j * HD + channel, side] = rows.astype(BF)


def second(where, pooled, w_qkv, mine, got, sizes, steps=1):
    nx, ny, nz = sizes
    half = HEADS // 2
    heads = half // steps
    value = pl.BlockSpec((heads, nx, HD, ny * nz), lambda i, *s: (i, 0, 0, 0))
    return pl.pallas_call(
        functools.partial(second_kernel, sizes=sizes),
        grid_spec=pltpu.PrefetchScalarGridSpec(
            num_scalar_prefetch=len(where),
            grid=(steps,),
            in_specs=[
                pl.BlockSpec(memory_space=pltpu.VMEM),
                pl.BlockSpec((C, 2 * C), lambda i, *s: (0, 0)),
                value,
                value,
            ],
            out_specs=[
                pl.BlockSpec((heads * HD, 2, nx, C), lambda i, *s: (i, 0, 0, 0)),
                pl.BlockSpec((ny + nz, C), lambda i, *s: (0, 0)),
                pl.BlockSpec((C, C), lambda i, *s: (0, 0)),
            ],
            scratch_shapes=[
                pltpu.VMEM((ny + 2 * nz, C), F32),
                pltpu.VMEM((heads, 2, nx * HD, C), F32),
            ],
        ),
        out_shape=[
            jax.ShapeDtypeStruct((half * HD, 2, nx, C), BF),
            jax.ShapeDtypeStruct((ny + nz, C), F32),
            jax.ShapeDtypeStruct((C, C), BF),
        ],
        name="second",
    )(*where, pooled, w_qkv, mine, got)


def middle_kernel(g_ref, kx_ref, out_ref):
    px, py, nx, _ = g_ref.shape
    lines = jnp.sum(g_ref[...].astype(F32), axis=1).reshape(px * nx, C)
    high = lines.astype(BF)
    low = (lines - high.astype(F32)).astype(BF)
    kx = kx_ref[...]
    mixed = dot(jnp.concatenate([kx, kx], axis=1), jnp.concatenate([high, low], axis=0))
    mixed = mixed.astype(BF).reshape(px, 1, nx, C)
    out_ref[...] = jnp.broadcast_to(mixed, out_ref.shape)


def middle(gathered, kx):
    vmem = pl.BlockSpec(memory_space=pltpu.VMEM)
    return pl.pallas_call(
        middle_kernel,
        in_specs=[vmem, vmem],
        out_specs=vmem,
        out_shape=jax.ShapeDtypeStruct(gathered.shape, BF),
        name="middle",
    )(gathered, kx)


def third_kernel(
    core_ref, q_ref, mine_ref, other_ref, tok_ref, wo_ref, wg_ref, wd_ref, out_ref, mix_scr, row_scr
):
    step = pl.program_id(0)
    nb, ny, nz, _ = tok_ref.shape
    nx = mix_scr.shape[0]
    half = HEADS // 2
    gz = core_ref[0]

    @pl.when(step == 0)
    def _():
        qy = q_ref[0:ny, :]
        qz = q_ref[ny : ny + nz, :]
        wides = []
        for head in (gz * half, (1 - gz) * half):
            wide_y = lane_expand(qy, head, half, False)
            wides.append((wide_y, lane_expand(qz, head, half, True)))
        for j in range(HEADS):
            source = mine_ref if j < half else other_ref
            head = jnp.where(gz == 0, j, (j + half) % HEADS)
            at = j % half * HD
            mixer = outer_yz(*wides[j // half], j % half)
            for i in range(2):
                rows = source[at : at + HD, i].astype(F32).reshape(HD * nx, C)
                row_scr[j, i] = rows
            narrow = jnp.concatenate(
                [
                    jnp.concatenate(
                        [row_scr[j, i, pl.ds(k, HD, stride=nx), :] for k in range(nx)], axis=0
                    )
                    for i in range(2)
                ],
                axis=1,
            ).astype(BF)
            mixed = dot(narrow, mixer, NT).astype(BF)
            mix_scr[:, head, :, :] = mixed.reshape(nx, HD, ny * nz)

    mixed = [mix_scr[step * nb + i].reshape(C, ny * nz).T for i in range(nb)]
    mixed = jnp.concatenate(mixed, axis=0)
    tok = tok_ref[...].reshape(nb * ny * nz, C)
    resid = tok.astype(F32) + dot(mixed, wo_ref[...])
    inner = norm_rows_matmul(resid).astype(BF)
    both = dot(inner, wg_ref[...]).astype(BF)
    gate = both[:, :FF]
    root = math.sqrt(2.0 / math.pi)
    inside = gate * (BF(root) + BF(root * 0.044715) * (gate * gate))
    half_gate = gate * BF(0.5)
    hidden = (half_gate + half_gate * jnp.tanh(inside)) * both[:, FF:]
    result = (resid + dot(hidden, wd_ref[...])).astype(BF)
    out_ref[...] = result.reshape(nb, ny, nz, C)


def third(core, q, mine, other, tokens, w_out, w_gate_up, w_down, block=2):
    nx, ny, nz, _ = tokens.shape
    full = lambda a: pl.BlockSpec(a.shape, lambda i, s: (0,) * a.ndim)
    slab = pl.BlockSpec((block, ny, nz, C), lambda i, s: (i, 0, 0, 0))
    vmem = pl.BlockSpec(memory_space=pltpu.VMEM)
    return pl.pallas_call(
        third_kernel,
        grid_spec=pltpu.PrefetchScalarGridSpec(
            num_scalar_prefetch=1,
            grid=(nx // block,),
            in_specs=[
                full(q),
                vmem,
                vmem,
                slab,
                full(w_out),
                full(w_gate_up),
                full(w_down),
            ],
            out_specs=slab,
            scratch_shapes=[
                pltpu.VMEM((nx, HEADS, HD, ny * nz), BF),
                pltpu.VMEM((HEADS, 2, nx * HD, C), F32),
            ],
        ),
        out_shape=jax.ShapeDtypeStruct(tokens.shape, BF),
        name="third",
    )(core, q, mine, other, tokens, w_out, w_gate_up, w_down)


def a2a(values, axes):
    return lax.all_to_all(values, axes, 0, 0, tiled=True)


def body(tokens, w_qkv, w_out, w_gate_up, w_down):
    nx, ny, nz, _ = tokens.shape
    cx, cy, cz = (lax.axis_size(a) for a in ("gx", "gy", "gz"))
    where = [lax.axis_index(a).astype(jnp.int32).reshape(1) for a in ("gx", "gy", "gz")]
    ry = ny // cx
    rz = nz // cx
    keep, send, pool, sum_x = first(where[2], tokens, w_qkv, cx)
    got_value = lax.ppermute(send, "gz", [(0, 1), (1, 0)])
    sum_x = sum_x.reshape(nx, C)
    pool, where = lax.optimization_barrier((pool, where))
    got = jnp.sum(a2a(pool, "gx"), axis=0)
    packed = jnp.concatenate([sum_x, got], axis=0)
    wide = jnp.broadcast_to(packed, (cy * cz,) + packed.shape)
    wide = a2a(wide, ("gy", "gz")).reshape(cy, cz, *packed.shape)
    total_x = jnp.sum(wide[:, :, :nx], axis=(0, 1))
    total_y = jnp.sum(wide[:, :, nx : nx + ry], axis=1).reshape(cy * ry, C)
    total_z = jnp.sum(wide[:, :, nx + ry : nx + ry + rz], axis=0).reshape(cz * rz, C)
    packed = jnp.concatenate([total_x, total_y, total_z], axis=0)
    packed, got_value = lax.optimization_barrier((packed, got_value))
    pooled = a2a(jnp.broadcast_to(packed, (cx,) + packed.shape), "gx")

    part, q, kx = second(where, pooled, w_qkv, keep, got_value, (nx, ny, nz))
    swap = [(0, 1), (1, 0)]
    gathered = a2a(part.reshape(cx * cy, nx, C), ("gx", "gy")).reshape(cx, cy, nx, C)
    spread = middle(gathered, kx).reshape(cx * cy, nx, C)
    mine = a2a(spread, ("gx", "gy")).reshape(part.shape)
    other = lax.ppermute(mine, "gz", swap)
    return third(where[2], q, mine, other, tokens, w_out, w_gate_up, w_down)


def solution(mesh):
    in_specs = (P("gx", "gy", "gz", None), P(), P(), P(), P())
    out_specs = P("gx", "gy", "gz", None)
    return jax.shard_map(body, mesh=mesh, in_specs=in_specs, out_specs=out_specs, check_vma=False)
```

```python
import functools
import math

import jax
import jax.numpy as jnp
from jax import lax
from jax.experimental import pallas as pl
from jax.experimental.pallas import tpu as pltpu
from jax.sharding import PartitionSpec as P

HEADS = 8
HD = 16
C = 128
FF = 512
EPS = 1e-05

BF = jnp.bfloat16
F32 = jnp.float32
NT = (((1,), (1,)), ((), ()))


def dot(a, b, dims=(((1,), (0,)), ((), ()))):
    return lax.dot_general(a, b, dims, preferred_element_type=F32)


def dot(a, b, dims=(((1,), (0,)), ((), ()))):
    return lax.dot_general(a, b, dims, preferred_element_type=F32)


def norm_rows(values):
    mean = jnp.mean(values, axis=-1, keepdims=True)
    centred = values - mean
    spread = jnp.mean(centred * centred, axis=-1, keepdims=True)
    return centred * lax.rsqrt(spread + EPS)


def halves(values):
    high = values.astype(BF)
    low = (values - high.astype(F32)).astype(BF)
    return jnp.concatenate([high, low], axis=1)


def twice(values):
    return jnp.concatenate([values, values], axis=0)


def norm_rows_matmul(values):
    centred = values - jnp.mean(values, axis=-1, keepdims=True)
    mean_of = jnp.full((C, C), 1.0 / C, BF)
    spread = dot((centred * centred).astype(BF), mean_of)
    return centred * lax.rsqrt(spread + EPS)


def iota2(shape, dim):
    return lax.broadcasted_iota(jnp.int32, shape, dim)


def ones_where(cond):
    return jnp.where(cond, 1.0, 0.0).astype(BF)


def first_kernel(
    core_ref, tok_ref, wv_ref, keep_ref, send_ref, pool_ref, sx_ref, sy_acc, sz_acc
):
    step = pl.program_id(0)
    nb, ny, nz, _ = tok_ref.shape
    x = tok_ref[...].reshape(nb * ny * nz, C).astype(F32)
    normed = norm_rows_matmul(x).astype(BF)
    wvt = wv_ref[...].T
    turned = jnp.concatenate([wvt[C // 2 :], wvt[: C // 2]], axis=0)
    wvt = jnp.where(core_ref[0] == 0, wvt, turned)
    n32 = normed.astype(F32).reshape(nb, ny, nz, C)
    sxy = jnp.sum(n32, axis=2)
    sy = jnp.sum(sxy, axis=0)
    sz = jnp.sum(jnp.sum(n32, axis=0), axis=0)
    sx_ref[0] = jnp.sum(sxy, axis=1)
    for i in range(nb):
        vt = dot(wvt, normed[i * ny * nz : (i + 1) * ny * nz], NT).astype(BF)
        shape = (HEADS // 2, HD, ny * nz)
        keep_ref[:, i, :, :] = vt[: C // 2].reshape(shape)
        send_ref[:, i, :, :] = vt[C // 2 :].reshape(shape)

    @pl.when(step == 0)
    def _():
        sy_acc[...] = jnp.zeros_like(sy_acc)
        sz_acc[...] = jnp.zeros_like(sz_acc)

    sy_acc[...] += sy
    sz_acc[...] += sz

    @pl.when(step == pl.num_programs(0) - 1)
    def _():
        parts = pool_ref.shape[0]
        ry = ny // parts
        rz = nz // parts
        pool_ref[...] = jnp.zeros_like(pool_ref)
        pool_ref[:, 0:ry, :] = sy_acc[...].reshape(parts, ry, C)
        pool_ref[:, ry : ry + rz, :] = sz_acc[...].reshape(parts, rz, C)


def first(core, tokens, w_qkv, parts, block=4):
    nx, ny, nz, _ = tokens.shape
    rows = -(-(ny // parts + nz // parts) // 8) * 8
    half = HEADS // 2
    value = pl.BlockSpec((half, block, HD, ny * nz), lambda i, s: (0, i, 0, 0))
    return pl.pallas_call(
        first_kernel,
        grid_spec=pltpu.PrefetchScalarGridSpec(
            num_scalar_prefetch=1,
            grid=(nx // block,),
            in_specs=[
                pl.BlockSpec((block, ny, nz, C), lambda i, s: (i, 0, 0, 0)),
                pl.BlockSpec((C, C), lambda i, s: (0, 2)),
            ],
            out_specs=[
                value,
                value,
                pl.BlockSpec((parts, rows, C), lambda i, s: (0, 0, 0)),
                pl.BlockSpec((1, block, C), lambda i, s: (i, 0, 0)),
            ],
            scratch_shapes=[pltpu.VMEM((ny, C), F32), pltpu.VMEM((nz, C), F32)],
        ),
        out_shape=[
            jax.ShapeDtypeStruct((half, nx, HD, ny * nz), BF),
            jax.ShapeDtypeStruct((half, nx, HD, ny * nz), BF),
            jax.ShapeDtypeStruct((parts, rows, C), F32),
            jax.ShapeDtypeStruct((nx // block, block, C), F32),
        ],
        name="first",
    )(core, tokens, w_qkv)


def lane_expand(rows, first_head, heads, fine):
    shape = (C, heads * HD * HD)
    col = iota2(shape, 1)
    pick = (col % HD) if fine else (col % (HD * HD) // HD)
    channel = (first_head + col // (HD * HD)) * HD + pick
    return dot(halves(rows), twice(ones_where(iota2(shape, 0) == channel)))


def outer_yz(wide_y, wide_z, at):
    ny, nz = wide_y.shape[0], wide_z.shape[0]
    cut = slice(at * HD * HD, (at + 1) * HD * HD)
    both = wide_y[:, cut].reshape(ny, 1, HD * HD) * wide_z[:, cut].reshape(1, nz, HD * HD)
    return both.reshape(ny * nz, HD * HD).astype(BF)


def second_kernel(
    x_ref,
    y_ref,
    core_ref,
    r_ref,
    w_ref,
    mine_ref,
    got_ref,
    out_ref,
    qo_ref,
    kx_ref,
    k_scr,
    row_scr,
    *,
    sizes
):
    step = pl.program_id(0)
    nx, ny, nz = sizes
    px, rows, _ = r_ref.shape
    gx, gy, gz = x_ref[0], y_ref[0], core_ref[0]
    ry = ny // px
    rz = nz // px
    pz = 2
    py = (rows - nx - pz * rz) // ry
    half = HEADS // pz

    @pl.when(step == 0)
    def _():
        pooled = r_ref[...].reshape(px * rows, C)
        qk = dot(halves(pooled), twice(w_ref[...])).reshape(px, rows, 2 * C)
        cuts = (0, nx, nx + py * ry, rows)
        scaled = []
        for axis in range(3):
            part = qk[:, cuts[axis] : cuts[axis + 1], :]
            length = px * (cuts[axis + 1] - cuts[axis])
            total = jnp.sum(jnp.sum(part * part, axis=0), axis=0, keepdims=True)
            mean_q = jnp.sum(total[:, :C], axis=1, keepdims=True) / (length * C)
            mean_k = jnp.sum(total[:, C:], axis=1, keepdims=True) / (length * C)
            root = 1.0 / math.sqrt(HD * length)
            scaled.append((lax.rsqrt(mean_q + 1e-06) * root, lax.rsqrt(mean_k + 1e-06)))
        all_x = qk[:, 0:nx, :].reshape(px * nx, 2 * C)
        owned = gz * half + gx // (px // half)
        query = all_x[:, :C] * scaled[0][0]
        key_part = all_x[:, C:] * scaled[0][1]
        key_part = jnp.where(iota2(key_part.shape, 1) // HD == owned, key_part, 0.0)
        q_terms, k_terms = halves(query), halves(key_part)
        q_terms = jnp.concatenate([q_terms, q_terms[:, :C]], axis=1)
        k_terms = jnp.concatenate([k_terms[:, :C], k_terms[:, :C], k_terms[:, C:]], axis=1)
        kx_ref[...] = dot(q_terms, k_terms, NT).astype(BF)
        own_y = jnp.zeros((px, ry, 2 * C), F32)
        for g in range(py):
            at = nx + g * ry
            own_y = jnp.where(gy == g, qk[:, at : at + ry, :], own_y)
        own_y = own_y.reshape(ny, 2 * C)
        at = nx + py * ry
        low = qk[:, at : at + rz, :].reshape(nz, 2 * C)
        high = qk[:, at + rz : at + 2 * rz, :].reshape(nz, 2 * C)
        own_z = jnp.where(gz == 0, low, high)
        other_z = jnp.where(gz == 0, high, low)
        qo_ref[0:ny, :] = own_y[:, :C] * scaled[1][0]
        qo_ref[ny:, :] = own_z[:, :C] * scaled[2][0]
        k_scr[0:ny, :] = own_y[:, C:] * scaled[1][1]
        k_scr[ny : ny + nz, :] = own_z[:, C:] * scaled[2][1]
        k_scr[ny + nz :, :] = other_z[:, C:] * scaled[2][1]

    heads = mine_ref.shape[0]
    first_head = gz * half + step * heads
    wide_y = lane_expand(k_scr[0:ny, :], first_head, heads, False)
    wide_z = lane_expand(k_scr[ny:, :], first_head, heads, True)
    for j in range(heads):
        narrow = jnp.zeros((nx * HD, HD * HD), F32)
        for i, source in enumerate((mine_ref, got_ref)):
            mixer = outer_yz(wide_y, wide_z[i * nz : (i + 1) * nz], j)
            narrow = narrow + dot(source[j].reshape(nx * HD, ny * nz), mixer)
        for side in range(2):
            row_scr[j, side] = narrow[:, side * C : (side + 1) * C]
            for channel in range(HD):
                rows = row_scr[j, side, pl.ds(channel, nx, stride=HD), :]
                out_ref[j * HD + channel, side] = rows.astype(BF)


def second(where, pooled, w_qkv, mine, got, sizes, steps=1):
    nx, ny, nz = sizes
    half = HEADS // 2
    heads = half // steps
    value = pl.BlockSpec((heads, nx, HD, ny * nz), lambda i, *s: (i, 0, 0, 0))
    return pl.pallas_call(
        functools.partial(second_kernel, sizes=sizes),
        grid_spec=pltpu.PrefetchScalarGridSpec(
            num_scalar_prefetch=len(where),
            grid=(steps,),
            in_specs=[
                pl.BlockSpec(memory_space=pltpu.VMEM),
                pl.BlockSpec((C, 2 * C), lambda i, *s: (0, 0)),
                value,
                value,
            ],
            out_specs=[
                pl.BlockSpec((heads * HD, 2, nx, C), lambda i, *s: (i, 0, 0, 0)),
                pl.BlockSpec((ny + nz, C), lambda i, *s: (0, 0)),
                pl.BlockSpec((C, C), lambda i, *s: (0, 0)),
            ],
            scratch_shapes=[
                pltpu.VMEM((ny + 2 * nz, C), F32),
                pltpu.VMEM((heads, 2, nx * HD, C), F32),
            ],
        ),
        out_shape=[
            jax.ShapeDtypeStruct((half * HD, 2, nx, C), BF),
            jax.ShapeDtypeStruct((ny + nz, C), F32),
            jax.ShapeDtypeStruct((C, C), BF),
        ],
        name="second",
    )(*where, pooled, w_qkv, mine, got)


def middle_kernel(g_ref, kx_ref, out_ref):
    px, py, nx, _ = g_ref.shape
    lines = jnp.sum(g_ref[...].astype(F32), axis=1).reshape(px * nx, C)
    high = lines.astype(BF)
    low = (lines - high.astype(F32)).astype(BF)
    kx = kx_ref[...]
    mixed = dot(jnp.concatenate([kx, kx], axis=1), jnp.concatenate([high, low], axis=0))
    mixed = mixed.astype(BF).reshape(px, 1, nx, C)
    out_ref[...] = jnp.broadcast_to(mixed, out_ref.shape)


def middle(gathered, kx):
    vmem = pl.BlockSpec(memory_space=pltpu.VMEM)
    return pl.pallas_call(
        middle_kernel,
        in_specs=[vmem, vmem],
        out_specs=vmem,
        out_shape=jax.ShapeDtypeStruct(gathered.shape, BF),
        name="middle",
    )(gathered, kx)


def third_kernel(
    core_ref, q_ref, mine_ref, other_ref, tok_ref, wo_ref, wg_ref, wd_ref, out_ref, mix_scr, row_scr
):
    step = pl.program_id(0)
    nb, ny, nz, _ = tok_ref.shape
    nx = mix_scr.shape[0]
    half = HEADS // 2
    gz = core_ref[0]

    @pl.when(step == 0)
    def _():
        qy = q_ref[0:ny, :]
        qz = q_ref[ny : ny + nz, :]
        wides = []
        for head in (gz * half, (1 - gz) * half):
            wide_y = lane_expand(qy, head, half, False)
            wides.append((wide_y, lane_expand(qz, head, half, True)))
        for j in range(HEADS):
            source = mine_ref if j < half else other_ref
            head = jnp.where(gz == 0, j, (j + half) % HEADS)
            at = j % half * HD
            mixer = outer_yz(*wides[j // half], j % half)
            for i in range(2):
                rows = source[at : at + HD, i].astype(F32).reshape(HD * nx, C)
                row_scr[j, i] = rows
            narrow = jnp.concatenate(
                [
                    jnp.concatenate(
                        [row_scr[j, i, pl.ds(k, HD, stride=nx), :] for k in range(nx)], axis=0
                    )
                    for i in range(2)
                ],
                axis=1,
            ).astype(BF)
            mixed = dot(narrow, mixer, NT).astype(BF)
            mix_scr[:, head, :, :] = mixed.reshape(nx, HD, ny * nz)

    mixed = [mix_scr[step * nb + i].reshape(C, ny * nz).T for i in range(nb)]
    mixed = jnp.concatenate(mixed, axis=0)
    tok = tok_ref[...].reshape(nb * ny * nz, C)
    resid = tok.astype(F32) + dot(mixed, wo_ref[...])
    inner = norm_rows_matmul(resid).astype(BF)
    both = dot(inner, wg_ref[...]).astype(BF)
    gate = both[:, :FF]
    root = math.sqrt(2.0 / math.pi)
    inside = gate * (BF(root) + BF(root * 0.044715) * (gate * gate))
    hidden = (gate + gate * jnp.tanh(inside)) * both[:, FF:]
    result = (resid + dot(hidden, wd_ref[...] * BF(0.5))).astype(BF)
    out_ref[...] = result.reshape(nb, ny, nz, C)


def third(core, q, mine, other, tokens, w_out, w_gate_up, w_down, block=2):
    nx, ny, nz, _ = tokens.shape
    full = lambda a: pl.BlockSpec(a.shape, lambda i, s: (0,) * a.ndim)
    slab = pl.BlockSpec((block, ny, nz, C), lambda i, s: (i, 0, 0, 0))
    vmem = pl.BlockSpec(memory_space=pltpu.VMEM)
    return pl.pallas_call(
        third_kernel,
        grid_spec=pltpu.PrefetchScalarGridSpec(
            num_scalar_prefetch=1,
            grid=(nx // block,),
            in_specs=[
                full(q),
                vmem,
                vmem,
                slab,
                full(w_out),
                full(w_gate_up),
                full(w_down),
            ],
            out_specs=slab,
            scratch_shapes=[
                pltpu.VMEM((nx, HEADS, HD, ny * nz), BF),
                pltpu.VMEM((HEADS, 2, nx * HD, C), F32),
            ],
        ),
        out_shape=jax.ShapeDtypeStruct(tokens.shape, BF),
        name="third",
    )(core, q, mine, other, tokens, w_out, w_gate_up, w_down)


def a2a(values, axes):
    return lax.all_to_all(values, axes, 0, 0, tiled=True)


def body(tokens, w_qkv, w_out, w_gate_up, w_down):
    nx, ny, nz, _ = tokens.shape
    cx, cy, cz = (lax.axis_size(a) for a in ("gx", "gy", "gz"))
    where = [lax.axis_index(a).astype(jnp.int32).reshape(1) for a in ("gx", "gy", "gz")]
    ry = ny // cx
    rz = nz // cx
    keep, send, pool, sum_x = first(where[2], tokens, w_qkv, cx)
    got_value = lax.ppermute(send, "gz", [(0, 1), (1, 0)])
    sum_x = sum_x.reshape(nx, C)
    pool, where = lax.optimization_barrier((pool, where))
    got = jnp.sum(a2a(pool, "gx"), axis=0)
    packed = jnp.concatenate([sum_x, got], axis=0)
    wide = jnp.broadcast_to(packed, (cy * cz,) + packed.shape)
    wide = a2a(wide, ("gy", "gz")).reshape(cy, cz, *packed.shape)
    total_x = jnp.sum(wide[:, :, :nx], axis=(0, 1))
    total_y = jnp.sum(wide[:, :, nx : nx + ry], axis=1).reshape(cy * ry, C)
    total_z = jnp.sum(wide[:, :, nx + ry : nx + ry + rz], axis=0).reshape(cz * rz, C)
    packed = jnp.concatenate([total_x, total_y, total_z], axis=0)
    packed, got_value = lax.optimization_barrier((packed, got_value))
    pooled = a2a(jnp.broadcast_to(packed, (cx,) + packed.shape), "gx")

    part, q, kx = second(where, pooled, w_qkv, keep, got_value, (nx, ny, nz))
    swap = [(0, 1), (1, 0)]
    gathered = a2a(part.reshape(cx * cy, nx, C), ("gx", "gy")).reshape(cx, cy, nx, C)
    spread = middle(gathered, kx).reshape(cx * cy, nx, C)
    mine = a2a(spread, ("gx", "gy")).reshape(part.shape)
    other = lax.ppermute(mine, "gz", swap)
    return third(where[2], q, mine, other, tokens, w_out, w_gate_up, w_down)


def solution(mesh):
    in_specs = (P("gx", "gy", "gz", None), P(), P(), P(), P())
    out_specs = P("gx", "gy", "gz", None)
    return jax.shard_map(body, mesh=mesh, in_specs=in_specs, out_specs=out_specs, check_vma=False)
```
